32 devices in a mesh: dp: 16 (over z, y, core), mp: 2 (over x).
Axes of the slice: x: 2, y: 2, z: 4, core: 2. Of those that a mesh axis runs over, the one named last changes fastest.
Arguments:
- tokens: bfloat16 [8000, 1024], P('dp'), may hold values from -6 to 6
- keep_mask: int32 [160, 50], P('dp'), may hold values from 0 to 1, as said below
- ln1_gain: float32 [1024], replicated, may hold values from 0.5 to 1.5
- ln1_bias: float32 [1024], replicated, may hold values from -1.75 to 1.75
- w_qkv: bfloat16 [1024, 3, 1024], P(None, None, 'mp'), may hold values from -0.1875 to 0.1875
- b_qkv: float32 [2, 1024], P(None, 'mp'), may hold values from -3 to 3
- w_proj: bfloat16 [1024, 1024], P('mp'), may hold values from -1 to 1
- b_proj: float32 [1024], replicated, may hold values from -1.75 to 1.75
- ln2_gain: float32 [1024], replicated, may hold values from 0.5 to 1.5
- ln2_bias: float32 [1024], replicated, may hold values from -1.75 to 1.75
- w_fc1: bfloat16 [1024, 4096], P(None, 'mp'), may hold values from -0.1875 to 0.1875
- b_fc1: float32 [4096], P('mp'), may hold values from -3 to 3
- w_fc2: bfloat16 [4096, 1024], P('mp'), may hold values from -0.09375 to 0.09375
- b_fc2: float32 [1024], replicated, may hold values from -1.75 to 1.75
- cotangent: bfloat16 [8000, 1024], P('dp'), may hold values from -6 to 6
Outputs:
- layer_out: bfloat16 [8000, 1024], P('dp')
- grad_tokens: bfloat16 [8000, 1024], P('dp')
- grad_ln1_gain: float32 [1024], replicated
- grad_ln1_bias: float32 [1024], replicated
- grad_w_qkv: float32 [1024, 3, 1024], P(None, None, 'mp')
- grad_b_qkv: float32 [2, 1024], P(None, 'mp')
- grad_w_proj: float32 [1024, 1024], P('mp')
- grad_b_proj: float32 [1024], replicated
- grad_ln2_gain: float32 [1024], replicated
- grad_ln2_bias: float32 [1024], replicated
- grad_w_fc1: float32 [1024, 4096], P(None, 'mp')
- grad_b_fc1: float32 [4096], P('mp')
- grad_w_fc2: float32 [4096, 1024], P('mp')
- grad_b_fc2: float32 [1024], replicated
The draws below stay inside these ranges and needn't reach their ends.
Inputs may be any that keep to these rules, and one draw needn't show every extreme that they name: `keep_mask`: each image keeps 25 to 50 slots; some image keeps exactly 25 and some all 50.
All inputs are finite; a program needn't handle non-finite values.
Results may differ from the reference program's by a relative error of at most 0.012.
Values sent between devices are 32-bit elements; how exact they have to be, the bound alone decides.
A program may use at most 192 MiB of HBM per device.

```python
import jax
import jax.numpy as jnp
from jax import lax

D = 1024
HEADS = 16
HEAD = 64
FF = 4096
SLOTS = 50
IMG_DEV = 10
IMAGES = 160
TOKENS = 8000
N_DP = 16


def draw_keep_mask(key, part):
    counts = jax.random.randint(jax.random.fold_in(key, 11), (IMAGES,), 25, SLOTS + 1)
    image_ids = jnp.arange(IMAGES)
    counts = jnp.where(image_ids == 0, 25, jnp.where(image_ids == 1, SLOTS, counts))
    base = jnp.tile(jnp.arange(SLOTS, dtype=jnp.int32)[None, :], (IMAGES, 1))
    ranks = jax.random.permutation(jax.random.fold_in(key, 12), base, axis=1, independent=True)
    return (ranks < counts[:, None]).astype(jnp.int32)


def steps_of(key, dims, shards, smallest, largest):
    factor_of = 1.0
    for axis_at, parts in shards:
        steps = jax.random.uniform(jax.random.fold_in(jax.random.fold_in(key, 6), axis_at), (parts,), jnp.float32, smallest / len(shards), largest / len(shards))
        factor_of = factor_of * jnp.repeat(jnp.exp(steps), dims[axis_at] // parts).reshape((-1,) + (1,) * (len(dims) - 1 - axis_at))
    return factor_of


def normal_values(key, extent, scale, reach, pieces=(), kind=jnp.bfloat16):
    factor_of = steps_of(key, extent, pieces, -0.22, 0.18) if pieces else 1.0
    result = jax.random.normal(key, extent, jnp.float32) * scale * factor_of
    return jnp.minimum(jnp.maximum(result, -reach), reach).astype(kind)


def setup_inputs(seed: int = 0) -> dict:
    seeds = jax.random.split(jax.random.key(seed), 16)
    return {
        "tokens": normal_values(seeds[0], (TOKENS, D), 1.0, 6.0, ((0, 16),)),
        "keep_mask": draw_keep_mask(jax.random.fold_in(seeds[15], 71), 0),
        "ln1_gain": jnp.clip(jax.random.uniform(seeds[2], (D,), jnp.float32, 0.5, 1.5), 0.5, 1.5),
        "ln1_bias": normal_values(seeds[3], (D,), 0.3, 1.75, (), jnp.float32),
        "w_qkv": normal_values(seeds[4], (D, 3, D), D ** -0.5, 0.1875, ((2, 2),)),
        "b_qkv": normal_values(seeds[5], (2, D), 0.5, 3.0, ((1, 2),), jnp.float32),
        "w_proj": normal_values(seeds[6], (D, D), (D // 32) ** -0.5, 1.0, ((0, 2),)),
        "b_proj": normal_values(seeds[7], (D,), 0.3, 1.75, (), jnp.float32),
        "ln2_gain": jnp.clip(jax.random.uniform(seeds[8], (D,), jnp.float32, 0.5, 1.5), 0.5, 1.5),
        "ln2_bias": normal_values(seeds[9], (D,), 0.3, 1.75, (), jnp.float32),
        "w_fc1": normal_values(seeds[10], (D, FF), D ** -0.5, 0.1875, ((1, 2),)),
        "b_fc1": normal_values(seeds[11], (FF,), 0.5, 3.0, ((0, 2),), jnp.float32),
        "w_fc2": normal_values(seeds[12], (FF, D), FF ** -0.5, 0.09375, ((0, 2),)),
        "b_fc2": normal_values(seeds[13], (D,), 0.3, 1.75, (), jnp.float32),
        "cotangent": normal_values(seeds[14], (TOKENS, D), 1.0, 6.0, ((0, 16),)),
    }


@jax.custom_vjp
def low(v):
    return lax.optimization_barrier(v.astype(jnp.bfloat16)).astype(jnp.float32)

@jax.custom_vjp
def low_back(v):
    return v

def low_keep(v):
    return (low(v), None)

def low_pass(kept, grad):
    return (grad,)

def back_keep(v):
    return (v, None)

def back_low(kept, grad):
    return (low(grad),)
low.defvjp(low_keep, low_pass)
low_back.defvjp(back_keep, back_low)

def layer_norm(value, gain, shift):
    centered = value - lax.optimization_barrier(jnp.mean(value, axis=-1, keepdims=True))
    variance = lax.optimization_barrier(jnp.mean(centered * centered, axis=-1, keepdims=True))
    return centered * lax.rsqrt(variance + 1e-06) * gain + shift

def attend(packed):
    query, key_rows, value_rows, kept = packed
    highest = lax.Precision.HIGHEST
    scores = low_back(jnp.einsum('bqhd,bkhd->bhqk', query, key_rows, precision=highest) * 0.125)
    live = (kept > 0)[:, None, None, :]
    masked = jnp.where(live, scores, -1e+30)
    row_max = lax.optimization_barrier(jnp.max(masked, axis=-1, keepdims=True))
    exp_terms = jnp.where(live, jnp.exp(masked - row_max), 0.0)
    probs = low(exp_terms / lax.optimization_barrier(jnp.sum(exp_terms, axis=-1, keepdims=True)))
    return jnp.einsum('bhqk,bkhd->bqhd', probs, value_rows, precision=highest)

def reference(tokens, keep_mask, ln1_gain, ln1_bias, w_qkv, b_qkv, w_proj, b_proj, ln2_gain, ln2_bias, w_fc1, b_fc1, w_fc2, b_fc2, cotangent):
    highest = lax.Precision.HIGHEST
    grouped_mask = keep_mask.reshape(N_DP, IMG_DEV, SLOTS)

    def split_heads(array):
        return array.reshape(N_DP, IMG_DEV, SLOTS, HEADS, HEAD)

    def forward(inputs, gain_one, bias_one, weight_qkv, bias_qkv, weight_proj, bias_proj, gain_two, bias_two, weight_one, bias_fc_one, weight_two, bias_fc_two):
        tok_rows = inputs.shape[0]
        norm_one = low(layer_norm(inputs, gain_one, bias_one))
        projected = jnp.dot(norm_one, weight_qkv.reshape(D, 3 * D), precision=highest).reshape(tok_rows, 3, D)
        query = low(low_back(projected[:, 0] + bias_qkv[0]))
        keys = low(low_back(projected[:, 1]))
        values = low(low_back(projected[:, 2] + bias_qkv[1]))
        mixed = lax.map(jax.checkpoint(attend), (split_heads(query), split_heads(keys), split_heads(values), grouped_mask))
        heads_out = low(low_back(mixed.reshape(tok_rows, D)))
        after_attn = inputs + low_back(jnp.dot(heads_out, weight_proj, precision=highest)) + bias_proj
        norm_two = low(layer_norm(after_attn, gain_two, bias_two))
        pre_act = low_back(jnp.dot(norm_two, weight_one, precision=highest) + bias_fc_one)
        hidden = low(jax.nn.gelu(pre_act, approximate=False))
        return after_attn + low_back(jnp.dot(hidden, weight_two, precision=highest)) + bias_fc_two
    floats = (tokens.astype(jnp.float32), ln1_gain, ln1_bias, w_qkv.astype(jnp.float32), b_qkv, w_proj.astype(jnp.float32), b_proj, ln2_gain, ln2_bias, w_fc1.astype(jnp.float32), b_fc1, w_fc2.astype(jnp.float32), b_fc2)
    final, pullback = jax.vjp(forward, *floats)
    grads = pullback(cotangent.astype(jnp.float32))
    return (final.astype(jnp.bfloat16), grads[0].astype(jnp.bfloat16), grads[1], grads[2], grads[3], grads[4], grads[5], grads[6], grads[7], grads[8], grads[9], grads[10], grads[11], grads[12])
```

```python
import jax
import jax.numpy as jnp
from jax import lax
from jax.sharding import PartitionSpec as P

HEAD = 64
BF16 = jnp.bfloat16
F32 = jnp.float32


def dot_nn(left, right):
    return jnp.dot(left, right, preferred_element_type=F32)


def dot_tn(left, right):
    return lax.dot_general(left, right, (((0,), (0,)), ((), ())), preferred_element_type=F32)


def dot_nt(left, right):
    return lax.dot_general(left, right, (((1,), (1,)), ((), ())), preferred_element_type=F32)


def norm_parts(value):
    centered = value - jnp.mean(value, axis=-1, keepdims=True)
    variance = jnp.mean(centered * centered, axis=-1, keepdims=True)
    inverse = lax.rsqrt(variance + 1e-06)
    return centered * inverse, inverse


def norm_back(grad, normalized, inverse, gain):
    scaled = grad * gain
    mean_one = jnp.mean(scaled, axis=-1, keepdims=True)
    mean_two = jnp.mean(scaled * normalized, axis=-1, keepdims=True)
    return inverse * (scaled - mean_one - normalized * mean_two)


def swap(value, axis, size, mask):
    return lax.ppermute(value, axis, [(i, i ^ mask) for i in range(size)])


def take_half(value, bit):
    half = value.shape[0] // 2
    return lax.dynamic_slice_in_dim(value, bit * half, half, 0)


def halve(value, bits, masks, size):
    for mask in masks:
        bit = bits[mask]
        sent = swap(take_half(value, 1 - bit), "dp", size, mask)
        value = take_half(value, bit) + sent
    return value


def double(value, bits, masks, size):
    for mask in reversed(masks):
        other = swap(value, "dp", size, mask)
        first = bits[mask] == 0
        value = jnp.where(
            jnp.stack([first, ~first])[:, None, None], value[None], other[None]
        ).reshape(2 * value.shape[0], value.shape[1])
    return value


def make_body(n_dp, n_mp):
    masks = [1 << k for k in range(n_dp.bit_length() - 1)]

    def sum_mp(part):
        if n_mp == 2:
            return part + swap(part, "mp", 2, 1)
        return lax.psum(part, "mp")

    def body(
        tokens, keep_mask, ln1_gain, ln1_bias, w_qkv, b_qkv, w_proj, b_proj,
        ln2_gain, ln2_bias, w_fc1, b_fc1, w_fc2, b_fc2, cotangent,
    ):
        dp_at = lax.axis_index("dp")
        bits = {mask: (dp_at // mask) % 2 for mask in masks}
        order_y = masks
        order_z = masks[:1] + masks[2:] + masks[1:2]

        def sum_outer(left, right, split):
            total = []
            for start, stop, order in ((0, split, order_y), (split, left.shape[1], order_z)):
                if stop == start:
                    continue
                piece = left[:, start:stop]
                half = (stop - start) // 2
                bit = bits[order[0]]
                away = lax.dynamic_slice_in_dim(piece, (1 - bit) * half, half, 1)
                here = lax.dynamic_slice_in_dim(piece, bit * half, half, 1)
                got = swap(dot_tn(away, right), "dp", n_dp, order[0])
                value = dot_tn(here, right) + got
                value = halve(value, bits, order[1:], n_dp)
                total.append(double(value, bits, order, n_dp))
            return jnp.concatenate(total, axis=0) if len(total) > 1 else total[0]

        def sum_small(value):
            for mask in masks:
                value = value + swap(value, "dp", n_dp, mask)
            return value

        inputs = tokens.astype(F32)
        tok_rows, width = inputs.shape
        images = keep_mask.shape[0]
        slots = tok_rows // images
        cols = w_qkv.shape[2]
        heads = cols // HEAD
        shape = (images, slots, heads, HEAD)

        normal_one, inverse_one = norm_parts(inputs)
        norm_one = (normal_one * ln1_gain + ln1_bias).astype(BF16)
        weight = w_qkv.transpose(1, 0, 2)
        query = (dot_nn(norm_one, weight[0]) + b_qkv[0]).astype(BF16).reshape(shape)
        keys = dot_nn(norm_one, weight[1]).astype(BF16).reshape(shape)
        values = (dot_nn(norm_one, weight[2]) + b_qkv[1]).astype(BF16).reshape(shape)
        scores = jnp.einsum("bqhd,bkhd->bhqk", query, keys, preferred_element_type=F32) * 0.125
        live = (keep_mask > 0)[:, None, None, :]
        masked = jnp.where(live, scores, -1e30)
        row_max = jnp.max(masked, axis=-1, keepdims=True)
        exp_terms = jnp.where(live, jnp.exp(masked - row_max), 0.0)
        probs = exp_terms / jnp.sum(exp_terms, axis=-1, keepdims=True)
        probs_low = probs.astype(BF16)
        mixed = jnp.einsum("bhqk,bkhd->bqhd", probs_low, values, preferred_element_type=F32)
        heads_out = mixed.reshape(tok_rows, cols).astype(BF16)
        after_attn = inputs + sum_mp(dot_nn(heads_out, w_proj)) + b_proj

        normal_two, inverse_two = norm_parts(after_attn)
        norm_two = (normal_two * ln2_gain + ln2_bias).astype(BF16)
        pre_act = dot_nn(norm_two, w_fc1) + b_fc1
        hidden_f, gelu_back = jax.vjp(lambda v: jax.nn.gelu(v, approximate=False), pre_act)
        hidden = hidden_f.astype(BF16)
        grad_w_fc2 = sum_outer(hidden, cotangent, hidden.shape[1] * 5 // 8)
        grad_pre = gelu_back(dot_nt(cotangent, w_fc2))[0].astype(BF16)
        grad_norm_two = sum_mp(dot_nt(grad_pre, w_fc1))
        grad_w_fc1 = sum_outer(norm_two, grad_pre, width * 5 // 8)
        mlp_sum = sum_mp(dot_nn(hidden, w_fc2))
        layer_out = (after_attn + mlp_sum + b_fc2).astype(BF16)

        grad_out = cotangent.astype(F32)
        grad_mid = grad_out + norm_back(grad_norm_two, normal_two, inverse_two, ln2_gain)
        grad_mid_low = grad_mid.astype(BF16)
        grad_heads = dot_nt(grad_mid_low, w_proj).astype(BF16).reshape(shape)
        grad_w_proj = sum_outer(heads_out, grad_mid_low, cols)
        grad_probs = jnp.einsum("bqhd,bkhd->bhqk", grad_heads, values, preferred_element_type=F32)
        grad_values = jnp.einsum(
            "bhqk,bqhd->bkhd", probs_low, grad_heads, preferred_element_type=F32
        ).astype(BF16)
        inner = jnp.sum(probs * grad_probs, axis=-1, keepdims=True)
        grad_scores = (probs * (grad_probs - inner)).astype(BF16)
        grad_query = (
            jnp.einsum("bhqk,bkhd->bqhd", grad_scores, keys, preferred_element_type=F32) * 0.125
        ).astype(BF16)
        grad_keys = (
            jnp.einsum("bhqk,bqhd->bkhd", grad_scores, query, preferred_element_type=F32) * 0.125
        ).astype(BF16)
        grad_query = grad_query.reshape(tok_rows, cols)
        grad_keys = grad_keys.reshape(tok_rows, cols)
        grad_values = grad_values.reshape(tok_rows, cols)
        part = (
            dot_nt(grad_query, weight[0])
            + dot_nt(grad_keys, weight[1])
            + dot_nt(grad_values, weight[2])
        )
        grad_norm_one = sum_mp(part)
        grad_w_qkv = jnp.stack(
            [
                sum_outer(norm_one, grad_query, width),
                sum_outer(norm_one, grad_keys, 0),
                sum_outer(norm_one, grad_values, width * 3 // 4),
            ],
            axis=1,
        )
        grad_tokens = (
            grad_mid + norm_back(grad_norm_one, normal_one, inverse_one, ln1_gain)
        ).astype(BF16)

        early = sum_small(
            jnp.concatenate(
                [
                    jnp.sum(grad_out, axis=0),
                    jnp.sum(grad_norm_two * normal_two, axis=0),
                    jnp.sum(grad_norm_two, axis=0),
                    jnp.sum(grad_mid, axis=0),
                    jnp.sum(grad_pre.astype(F32), axis=0),
                    jnp.sum(grad_query.astype(F32), axis=0),
                    jnp.sum(grad_values.astype(F32), axis=0),
                ]
            ).reshape(-1, 128)
        ).reshape(-1)
        late = sum_small(
            jnp.concatenate(
                [jnp.sum(grad_norm_one * normal_one, axis=0), jnp.sum(grad_norm_one, axis=0)]
            ).reshape(-1, 128)
        ).reshape(-1)
        spot = 4 * width + b_fc1.shape[0]
        return (
            layer_out,
            grad_tokens,
            late[:width],
            late[width:],
            grad_w_qkv,
            early[spot:].reshape(2, cols),
            grad_w_proj,
            early[3 * width : 4 * width],
            early[width : 2 * width],
            early[2 * width : 3 * width],
            grad_w_fc1,
            early[4 * width : spot],
            grad_w_fc2,
            early[:width],
        )

    return body


def solution(mesh):
    return jax.shard_map(
        make_body(mesh.shape["dp"], mesh.shape["mp"]),
        mesh=mesh,
        in_specs=(
            P("dp", None),
            P("dp", None),
            P(),
            P(),
            P(None, None, "mp"),
            P(None, "mp"),
            P("mp", None),
            P(),
            P(),
            P(),
            P(None, "mp"),
            P("mp"),
            P("mp", None),
            P(),
            P("dp", None),
        ),
        out_specs=(
            P("dp", None),
            P("dp", None),
            P(),
            P(),
            P(None, None, "mp"),
            P(None, "mp"),
            P("mp", None),
            P(),
            P(),
            P(),
            P(None, "mp"),
            P("mp"),
            P("mp", None),
            P(),
        ),
        check_vma=False,
    )
```

```python
import functools

import jax
import jax.numpy as jnp
from jax import lax
from jax.experimental import pallas as pl
from jax.experimental.pallas import tpu as pltpu
from jax.sharding import PartitionSpec as P

HEAD = 64
BF16 = jnp.bfloat16
MESH = pl.DeviceIdType.MESH
F32 = jnp.float32


def dot_nn(left, right):
    return jnp.dot(left, right, preferred_element_type=F32)


def dot_tn(left, right):
    return lax.dot_general(left, right, (((0,), (0,)), ((), ())), preferred_element_type=F32)


def dot_nt(left, right):
    return lax.dot_general(left, right, (((1,), (1,)), ((), ())), preferred_element_type=F32)


def norm_parts(value):
    centered = value - jnp.mean(value, axis=-1, keepdims=True)
    variance = jnp.mean(centered * centered, axis=-1, keepdims=True)
    inverse = lax.rsqrt(variance + 1e-06)
    return centered * inverse, inverse


def norm_back(grad, normalized, inverse, gain):
    scaled = grad * gain
    mean_one = jnp.mean(scaled, axis=-1, keepdims=True)
    mean_two = jnp.mean(scaled * normalized, axis=-1, keepdims=True)
    return inverse * (scaled - mean_one - normalized * mean_two)


def swap(value, axis, size, mask):
    return lax.ppermute(value, axis, [(i, i ^ mask) for i in range(size)])


def plan(shapes, unit_bytes=1 << 20):
    out = []
    for rows, cols in shapes:
        count = max(1, rows * cols * 4 // 2 // unit_bytes)
        out.append((rows // 2 // count, cols, count))
    return out


def add_into(dst, src_a, src_b, rows):
    step = 16

    @pl.loop(0, rows // step)
    def _(i):
        at = pl.ds(pl.multiple_of(i * step, step), step)
        dst[at, :] = src_a[at, :] + src_b[at, :]


def sum_kernel(layout, offs, n_arr, *refs):
    ins = refs[:n_arr]
    outs = refs[n_arr : 2 * n_arr]
    rest = refs[2 * n_arr :]
    per = 10
    bufs = [rest[i * per : (i + 1) * per] for i in range(n_arr)]
    send_sem, recv_sem, load_sem, out_sem, away_sem, land_sem = rest[n_arr * per :]
    me, mp = lax.axis_index("dp"), lax.axis_index("mp")
    core, y, z = me % 2, (me // 2) % 2, me // 4
    to_core = (me + 1 - 2 * core, mp)
    to_y = (me + 2 - 4 * y, mp)
    to_z = (me + 4 - 8 * (z % 2), mp)
    to_mid = (me + 4 - 8 * ((z + 1) % 2), mp)
    center = z * (3 - z) > 0
    leaf = z * (3 - z) == 0
    upper = z // 2

    barrier = pltpu.get_barrier_semaphore()
    for target in (to_core, to_y, to_z):
        pl.semaphore_signal(barrier, inc=1, device_id=target, device_id_type=MESH)

    @pl.when(center)
    def _():
        pl.semaphore_signal(barrier, inc=1, device_id=to_mid, device_id_type=MESH)
        pl.semaphore_wait(barrier, 4)

    @pl.when(leaf)
    def _():
        pl.semaphore_wait(barrier, 3)

    def remote(src, dst, unit, stage, target):
        return pltpu.make_async_remote_copy(
            src_ref=src, dst_ref=dst, send_sem=send_sem.at[unit, stage], recv_sem=recv_sem.at[unit, stage],
            device_id=target, device_id_type=MESH,
        )

    actions = []
    finals = []
    unit_id = 0
    first = []
    order = []
    for a, (m, cols, count) in enumerate(layout):
        for j in range(count):
            order.append((a, j, 0))
            order.append((a, j, 1))
    p_seen = r_seen = 0
    for a, j, kind in order:
        m, cols, count = layout[a]
        n, h = m // 2, m // 4
        acc, got, y_in, z_in, m_in, a_in, rz_in, rm_in, ry_in, ra_in = bufs[a]
        g, o = ins[a], outs[a]
        base = (kind * count + j) * m
        slot = kind * count + j
        u = unit_id
        unit_id += 1
        mine = base + core * n
        theirs = base + (1 - core) * n
        acc_u = acc.at[slot]
        rows_at = lambda start, size: pl.ds(pl.multiple_of(start, 8), size)
        load = pltpu.make_async_copy(g.at[rows_at(mine, n), :], acc_u, load_sem.at[u])
        swap = remote(g.at[rows_at(theirs, n), :], got.at[slot], u, 0, to_core)
        first.append((load, swap))

        def start_sum(load=load, swap=swap, acc_u=acc_u, got_u=got.at[slot], n=n):
            load.wait()
            swap.wait_recv()
            add_into(acc_u, acc_u, got_u, n)

        def emit(src, at, size, idx, u=u, o=o):
            here = pltpu.make_async_copy(src, o.at[rows_at(at, size), :], out_sem.at[u, idx])
            there = pltpu.make_async_remote_copy(
                src_ref=src, dst_ref=o.at[rows_at(at, size), :], send_sem=away_sem.at[u, idx],
                recv_sem=land_sem.at[u, idx], device_id=to_core, device_id_type=MESH,
            )
            here.start()
            there.start()

            def end():
                here.wait()
                there.wait()

            return end

        if kind == 0:
            t0 = p_seen * offs["slot"]
            p_seen += 1
            keep, away = rows_at(y * h, h), rows_at((1 - y) * h, h)
            acc_k, acc_w = acc_u.at[keep], acc_u.at[away]
            ys = remote(acc_w, y_in.at[j], u, 1, to_y)
            up = remote(acc_k, z_in.at[j], u, 2, to_z)
            md = remote(acc_k, m_in.at[j], u, 3, to_mid)
            dn = remote(m_in.at[j], z_in.at[j], u, 4, to_z)
            ag_c = remote(m_in.at[j], a_in.at[j], u, 5, to_y)
            ag_l = remote(z_in.at[j], a_in.at[j], u, 5, to_y)

            def s0(start_sum=start_sum, ys=ys):
                start_sum()
                ys.start()

            def s1(ys=ys, up=up, acc_k=acc_k, y_u=y_in.at[j], h=h):
                ys.wait_recv()
                add_into(acc_k, acc_k, y_u, h)

                @pl.when(leaf)
                def _():
                    up.start()

            def s2(up=up, md=md, acc_k=acc_k, z_u=z_in.at[j], h=h):
                @pl.when(center)
                def _():
                    up.wait_recv()
                    add_into(acc_k, acc_k, z_u, h)
                    md.start()

            def s3(md=md, dn=dn, ag_c=ag_c, acc_k=acc_k, m_u=m_in.at[j], h=h):
                @pl.when(center)
                def _():
                    md.wait_recv()
                    add_into(m_u, acc_k, m_u, h)
                    dn.start()
                    ag_c.start()

            def s4(dn=dn, ag_l=ag_l):
                @pl.when(leaf)
                def _():
                    dn.wait_recv()
                    ag_l.start()

            def s5(dn=dn, up=up, md=md, ag_c=ag_c, ag_l=ag_l, ys=ys, swap=swap, mine=mine, h=h, j=j, m_in=m_in,
                   z_in=z_in, a_in=a_in, emit=emit):
                ag_c.wait_recv()
                end_a = emit(a_in.at[j], mine + (1 - y) * h, h, 1)

                @pl.when(center)
                def _():
                    emit(m_in.at[j], mine + y * h, h, 0)

                @pl.when(leaf)
                def _():
                    emit(z_in.at[j], mine + y * h, h, 0)

                def end():
                    end_a()
                    src = m_in.at[j]
                    o = outs_of
                    swap.wait_send()
                    ys.wait_send()
                    ag_c.wait_send()

                    @pl.when(leaf)
                    def _():
                        up.wait_send()

                    @pl.when(center)
                    def _():
                        md.wait_send()
                        dn.wait_send()

                outs_of = None
                return end

            def wait_final(u=u, o=o, m_in=m_in, j=j, mine=mine, h=h):
                pltpu.make_async_copy(m_in.at[j], o.at[rows_at(mine + y * h, h), :], out_sem.at[u, 0]).wait()
                pltpu.make_async_remote_copy(
                    src_ref=m_in.at[j], dst_ref=o.at[rows_at(mine + y * h, h), :], send_sem=away_sem.at[u, 0],
                    recv_sem=land_sem.at[u, 0], device_id=to_core, device_id_type=MESH,
                ).wait()

            for k, s in enumerate((s0, s1, s2, s3, s4)):
                actions.append((t0 + offs["p"][k], len(actions), s))

            def s5w(s5=s5, wait_final=wait_final):
                end = s5()
                finals.append(end)
                finals.append(wait_final)

            actions.append((t0 + offs["p"][5], len(actions), s5w))
        else:
            t0 = r_seen * offs["slot"] + offs["lag"]
            r_seen += 1
            own, oth = rows_at(upper * h, h), rows_at((1 - upper) * h, h)
            acc_o, acc_t = acc_u.at[own], acc_u.at[oth]
            up = remote(acc_u, rz_in.at[j], u, 1, to_z)
            md = remote(acc_t, rm_in.at[j], u, 2, to_mid)
            ys = remote(acc_o, ry_in.at[j], u, 3, to_y)
            ma = remote(ry_in.at[j], ra_in.at[j], u, 4, to_mid)
            d0 = remote(ry_in.at[j], rz_in.at[j].at[own], u, 5, to_z)
            d1 = remote(ra_in.at[j], rz_in.at[j].at[oth], u, 6, to_z)

            def s0(start_sum=start_sum, up=up):
                start_sum()

                @pl.when(leaf)
                def _():
                    up.start()

            def s1(up=up, md=md, acc_u=acc_u, z_u=rz_in.at[j], n=n):
                @pl.when(center)
                def _():
                    up.wait_recv()
                    add_into(acc_u, acc_u, z_u, n)
                    md.start()

            def s2(md=md, ys=ys, acc_o=acc_o, m_u=rm_in.at[j], h=h):
                @pl.when(center)
                def _():
                    md.wait_recv()
                    add_into(acc_o, acc_o, m_u, h)
                    ys.start()

            def s3(ys=ys, ma=ma, d0=d0, acc_o=acc_o, y_u=ry_in.at[j], h=h, emit=emit, mine=mine):
                @pl.when(center)
                def _():
                    ys.wait_recv()
                    add_into(y_u, acc_o, y_u, h)
                    ma.start()
                    d0.start()
                    emit(y_u, mine + upper * h, h, 0)

            def s4(ma=ma, d1=d1, ra_u=ra_in.at[j], emit=emit, mine=mine, h=h):
                @pl.when(center)
                def _():
                    ma.wait_recv()
                    d1.start()
                    emit(ra_u, mine + (1 - upper) * h, h, 1)

            def s5(d0=d0, d1=d1, z_u=rz_in.at[j], emit=emit, mine=mine, h=h, own=own, oth=oth):
                @pl.when(leaf)
                def _():
                    d0.wait_recv()
                    emit(z_u.at[own], mine + upper * h, h, 0)
                    d1.wait_recv()
                    emit(z_u.at[oth], mine + (1 - upper) * h, h, 1)

            def s6(u=u, o=o, z_u=rz_in.at[j], mine=mine, h=h, swap=swap, up=up, md=md, ys=ys, ma=ma, d0=d0, d1=d1,
                   own=own, oth=oth):
                for idx, part, at in ((0, own, upper * h), (1, oth, (1 - upper) * h)):
                    pltpu.make_async_copy(z_u.at[part], o.at[rows_at(mine + at, h), :], out_sem.at[u, idx]).wait()
                    pltpu.make_async_remote_copy(
                        src_ref=z_u.at[part], dst_ref=o.at[rows_at(mine + at, h), :], send_sem=away_sem.at[u, idx],
                        recv_sem=land_sem.at[u, idx], device_id=to_core, device_id_type=MESH,
                    ).wait()
                swap.wait_send()

                @pl.when(leaf)
                def _():
                    up.wait_send()

                @pl.when(center)
                def _():
                    for c in (md, ys, ma, d0, d1):
                        c.wait_send()

            for k, s in enumerate((s0, s1, s2, s3, s4, s5)):
                actions.append((t0 + offs["r"][k], len(actions), s))
            finals.append(s6)

    for load, swap in first:
        load.start()
        swap.start()
    for _, _, act in sorted(actions, key=lambda t: t[:2]):
        act()
    for end in finals:
        end()


OFFS = {"slot": 1.0, "lag": 0.2, "p": (0, 1, 2, 3, 4, 5), "r": (0, 1.3, 2, 2.7, 3.4, 4.5)}


def sum_dp(arrays, offs=OFFS, unit_bytes=1 << 20):
    layout = plan([a.shape for a in arrays], unit_bytes)
    scratch = []
    units = 0
    for m, cols, count in layout:
        n, h = m // 2, m // 4
        units += 2 * count
        for c, r in ((2 * count, n), (2 * count, n), (count, h), (count, h), (count, h), (count, h),
                     (count, n), (count, h), (count, h), (count, h)):
            scratch.append(pltpu.VMEM((c, r, cols), F32))
    scratch += [
        pltpu.SemaphoreType.DMA((units, 7)), pltpu.SemaphoreType.DMA((units, 7)), pltpu.SemaphoreType.DMA((units,)),
        pltpu.SemaphoreType.DMA((units, 2)), pltpu.SemaphoreType.DMA((units, 2)), pltpu.SemaphoreType.DMA((units, 2)),
    ]
    anyspec = pl.BlockSpec(memory_space=pl.ANY)
    return pl.pallas_call(
        functools.partial(sum_kernel, layout, offs, len(arrays)),
        out_shape=[jax.ShapeDtypeStruct(a.shape, F32) for a in arrays],
        in_specs=[anyspec] * len(arrays),
        out_specs=[anyspec] * len(arrays),
        scratch_shapes=scratch,
        name="sum_dp",
        compiler_params=pltpu.CompilerParams(collective_id=0, has_side_effects=True, vmem_limit_bytes=62 << 20),
    )(*arrays)


def small_kernel(value_ref, out_ref, got, send_sem, recv_sem):
    me, mp = lax.axis_index("dp"), lax.axis_index("mp")
    core, y, z = me % 2, (me // 2) % 2, me // 4
    targets = (
        me + 1 - 2 * core,
        me + 2 - 4 * y,
        me + 4 - 8 * (z % 2),
        me + 8 - 16 * (z // 2),
    )
    barrier = pltpu.get_barrier_semaphore()
    for target in targets:
        pl.semaphore_signal(barrier, inc=1, device_id=(target, mp), device_id_type=MESH)
    pl.semaphore_wait(barrier, 4)
    out_ref[...] = value_ref[...]
    src = value_ref
    for k, target in enumerate(targets):
        copy = pltpu.make_async_remote_copy(
            src_ref=src, dst_ref=got.at[k], send_sem=send_sem.at[k], recv_sem=recv_sem.at[k],
            device_id=(target, mp), device_id_type=MESH,
        )
        copy.start()
        copy.wait()
        if k < 3:
            got[4 + k] = src[...] + got[k]
            src = got.at[4 + k]
        else:
            out_ref[...] = src[...] + got[k]


def sum_dp_small(value):
    return pl.pallas_call(
        small_kernel,
        out_shape=jax.ShapeDtypeStruct(value.shape, F32),
        in_specs=[pl.BlockSpec(memory_space=pltpu.VMEM)],
        out_specs=pl.BlockSpec(memory_space=pltpu.VMEM),
        scratch_shapes=[
            pltpu.VMEM((7,) + value.shape, F32),
            pltpu.SemaphoreType.DMA((4,)),
            pltpu.SemaphoreType.DMA((4,)),
        ],
        name="sum_dp_small",
        compiler_params=pltpu.CompilerParams(collective_id=1, has_side_effects=True),
    )(value)


def make_body(n_dp, n_mp):
    fast = n_dp == 16 and n_mp == 2

    def sum_mp(part):
        if n_mp == 2:
            return part + swap(part, "mp", 2, 1)
        return lax.psum(part, "mp")

    def body(
        tokens, keep_mask, ln1_gain, ln1_bias, w_qkv, b_qkv, w_proj, b_proj,
        ln2_gain, ln2_bias, w_fc1, b_fc1, w_fc2, b_fc2, cotangent,
    ):
        inputs = tokens.astype(F32)
        tok_rows, width = inputs.shape
        images = keep_mask.shape[0]
        slots = tok_rows // images
        cols = w_qkv.shape[2]
        heads = cols // HEAD
        shape = (images, slots, heads, HEAD)

        normal_one, inverse_one = norm_parts(inputs)
        norm_one = (normal_one * ln1_gain + ln1_bias).astype(BF16)
        weight = w_qkv.transpose(1, 0, 2)
        query = (dot_nn(norm_one, weight[0]) + b_qkv[0]).astype(BF16).reshape(shape)
        keys = dot_nn(norm_one, weight[1]).astype(BF16).reshape(shape)
        values = (dot_nn(norm_one, weight[2]) + b_qkv[1]).astype(BF16).reshape(shape)
        scores = jnp.einsum("bqhd,bkhd->bhqk", query, keys, preferred_element_type=F32) * 0.125
        live = (keep_mask > 0)[:, None, None, :]
        masked = jnp.where(live, scores, -1e30)
        row_max = jnp.max(masked, axis=-1, keepdims=True)
        exp_terms = jnp.where(live, jnp.exp(masked - row_max), 0.0)
        probs = exp_terms / jnp.sum(exp_terms, axis=-1, keepdims=True)
        probs_low = probs.astype(BF16)
        mixed = jnp.einsum("bhqk,bkhd->bqhd", probs_low, values, preferred_element_type=F32)
        heads_out = mixed.reshape(tok_rows, cols).astype(BF16)
        after_attn = inputs + sum_mp(dot_nn(heads_out, w_proj)) + b_proj

        normal_two, inverse_two = norm_parts(after_attn)
        norm_two = (normal_two * ln2_gain + ln2_bias).astype(BF16)
        pre_act = dot_nn(norm_two, w_fc1) + b_fc1
        hidden_f, gelu_back = jax.vjp(lambda v: jax.nn.gelu(v, approximate=False), pre_act)
        hidden = hidden_f.astype(BF16)
        grad_w_fc2 = dot_tn(hidden, cotangent)
        grad_pre = gelu_back(dot_nt(cotangent, w_fc2))[0].astype(BF16)
        grad_norm_two = sum_mp(dot_nt(grad_pre, w_fc1))
        grad_w_fc1 = dot_tn(norm_two, grad_pre)
        mlp_sum = sum_mp(dot_nn(hidden, w_fc2))
        layer_out = (after_attn + mlp_sum + b_fc2).astype(BF16)

        grad_out = cotangent.astype(F32)
        grad_mid = grad_out + norm_back(grad_norm_two, normal_two, inverse_two, ln2_gain)
        grad_mid_low = grad_mid.astype(BF16)
        grad_heads = dot_nt(grad_mid_low, w_proj).astype(BF16).reshape(shape)
        grad_w_proj = dot_tn(heads_out, grad_mid_low)
        grad_probs = jnp.einsum("bqhd,bkhd->bhqk", grad_heads, values, preferred_element_type=F32)
        grad_values = jnp.einsum(
            "bhqk,bqhd->bkhd", probs_low, grad_heads, preferred_element_type=F32
        ).astype(BF16)
        inner = jnp.sum(probs * grad_probs, axis=-1, keepdims=True)
        grad_scores = (probs * (grad_probs - inner)).astype(BF16)
        grad_query = (
            jnp.einsum("bhqk,bkhd->bqhd", grad_scores, keys, preferred_element_type=F32) * 0.125
        ).astype(BF16)
        grad_keys = (
            jnp.einsum("bhqk,bqhd->bkhd", grad_scores, query, preferred_element_type=F32) * 0.125
        ).astype(BF16)
        grad_query = grad_query.reshape(tok_rows, cols)
        grad_keys = grad_keys.reshape(tok_rows, cols)
        grad_values = grad_values.reshape(tok_rows, cols)
        part = (
            dot_nt(grad_query, weight[0])
            + dot_nt(grad_keys, weight[1])
            + dot_nt(grad_values, weight[2])
        )
        grad_norm_one = sum_mp(part)
        grads = [
            grad_w_fc2,
            grad_w_fc1,
            grad_w_proj,
            dot_tn(norm_one, grad_values),
            dot_tn(norm_one, grad_query),
            dot_tn(norm_one, grad_keys),
        ]
        if fast:
            grads = sum_dp(grads)
        else:
            grads = lax.psum(grads, "dp")
        grad_w_fc2, grad_w_fc1, grad_w_proj, grad_w_v, grad_w_q, grad_w_k = grads
        grad_w_qkv = jnp.stack([grad_w_q, grad_w_k, grad_w_v], axis=1)
        grad_tokens = (
            grad_mid + norm_back(grad_norm_one, normal_one, inverse_one, ln1_gain)
        ).astype(BF16)

        small = jnp.concatenate(
            [
                jnp.sum(grad_out, axis=0),
                jnp.sum(grad_norm_two * normal_two, axis=0),
                jnp.sum(grad_norm_two, axis=0),
                jnp.sum(grad_mid, axis=0),
                jnp.sum(grad_norm_one * normal_one, axis=0),
                jnp.sum(grad_norm_one, axis=0),
                jnp.sum(grad_pre.astype(F32), axis=0),
                jnp.sum(grad_query.astype(F32), axis=0),
                jnp.sum(grad_values.astype(F32), axis=0),
            ]
        )
        if fast:
            small = sum_dp_small(small.reshape(-1, 128)).reshape(-1)
        else:
            small = lax.psum(small, "dp")
        rows = [small[k * width : (k + 1) * width] for k in range(6)]
        spot = 6 * width + b_fc1.shape[0]
        return (
            layer_out,
            grad_tokens,
            rows[4],
            rows[5],
            grad_w_qkv,
            small[spot:].reshape(2, cols),
            grad_w_proj,
            rows[3],
            rows[1],
            rows[2],
            grad_w_fc1,
            small[6 * width : spot],
            grad_w_fc2,
            rows[0],
        )

    return body


def solution(mesh):
    return jax.shard_map(
        make_body(mesh.shape["dp"], mesh.shape["mp"]),
        mesh=mesh,
        in_specs=(
            P("dp", None),
            P("dp", None),
            P(),
            P(),
            P(None, None, "mp"),
            P(None, "mp"),
            P("mp", None),
            P(),
            P(),
            P(),
            P(None, "mp"),
            P("mp"),
            P("mp", None),
            P(),
            P("dp", None),
        ),
        out_specs=(
            P("dp", None),
            P("dp", None),
            P(),
            P(),
            P(None, None, "mp"),
            P(None, "mp"),
            P("mp", None),
            P(),
            P(),
            P(),
            P(None, "mp"),
            P("mp"),
            P("mp", None),
            P(),
        ),
        check_vma=False,
    )
```

```python
import functools

import jax
import jax.numpy as jnp
from jax import lax
from jax.experimental import pallas as pl
from jax.experimental.pallas import tpu as pltpu
from jax.sharding import PartitionSpec as P

HEAD = 64
BF16 = jnp.bfloat16
MESH = pl.DeviceIdType.MESH
F32 = jnp.float32


def dot_nn(left, right):
    return jnp.dot(left, right, preferred_element_type=F32)


def dot_tn(left, right):
    return lax.dot_general(left, right, (((0,), (0,)), ((), ())), preferred_element_type=F32)


def dot_nt(left, right):
    return lax.dot_general(left, right, (((1,), (1,)), ((), ())), preferred_element_type=F32)


def norm_parts(value):
    centered = value - jnp.mean(value, axis=-1, keepdims=True)
    variance = jnp.mean(centered * centered, axis=-1, keepdims=True)
    inverse = lax.rsqrt(variance + 1e-06)
    return centered * inverse, inverse


def norm_back(grad, normalized, inverse, gain):
    scaled = grad * gain
    mean_one = jnp.mean(scaled, axis=-1, keepdims=True)
    mean_two = jnp.mean(scaled * normalized, axis=-1, keepdims=True)
    return inverse * (scaled - mean_one - normalized * mean_two)


def swap(value, axis, size, mask):
    return lax.ppermute(value, axis, [(i, i ^ mask) for i in range(size)])


def split_plan(shapes, unit_bytes=1 << 20):
    out = []
    for rows, cols in shapes:
        count = max(1, rows * cols * 4 // 2 // unit_bytes)
        out.append((rows // 2 // count, cols, count))
    return out


def rows_at(start, size):
    return pl.ds(pl.multiple_of(start, 8), size)


def each_block(total, step, body, carry=()):
    full = total // step
    if full:
        carry = lax.fori_loop(
            0, full, lambda i, c: body(pl.ds(pl.multiple_of(i * step, step), step), c), carry
        )
    if total % step:
        carry = body(pl.ds(full * step, total % step), carry)
    return carry


def add_into(dst, src_a, src_b):
    @pl.loop(0, dst.shape[0] // 16)
    def _(i):
        at = pl.ds(pl.multiple_of(i * 16, 16), 16)
        dst[at, :] = src_a[at, :] + src_b[at, :]


def fold(value):
    return jnp.sum(value, axis=0, keepdims=True)


def norm_back_rows(value, grad, gain):
    normal, inverse = norm_parts(value)
    return normal, norm_back(grad, normal, inverse, gain)


def attend_back(q, k, v, g, live, first):
    grad_q = grad_k = grad_v = None
    for own in (first, 1 - first):
        own = own.astype(BF16)
        q_own, g_own, k_own = q * own, g * own, k * own
        scores = jnp.where(live, dot_nt(q_own, k) * 0.125, -1e30)
        exp_terms = jnp.where(live, jnp.exp(scores - jnp.max(scores, axis=-1, keepdims=True)), 0.0)
        probs = exp_terms / jnp.maximum(jnp.sum(exp_terms, axis=-1, keepdims=True), 1.0)
        grad_probs = dot_nt(g_own, v)
        inner = jnp.sum(probs * grad_probs, axis=-1, keepdims=True)
        grad_scores = (probs * (grad_probs - inner)).astype(BF16)
        parts = (dot_nn(grad_scores, k_own), dot_tn(grad_scores, q_own), dot_tn(probs.astype(BF16), g_own))
        if grad_q is None:
            grad_q, grad_k, grad_v = parts
        else:
            grad_q, grad_k, grad_v = grad_q + parts[0], grad_k + parts[1], grad_v + parts[2]
    return (grad_q * 0.125).astype(BF16), (grad_k * 0.125).astype(BF16), grad_v.astype(BF16)


BUFFERS = 7


def back_kernel(layout, keys, slots, group, *refs):
    (g_fc2, g_fc1, near_hbm, mlp_hbm, after_hbm, tok_hbm, cot_hbm, q_hbm, k_hbm, v_hbm, live_hbm, wproj_hbm,
     wqkv_hbm, n1t_hbm, ht_hbm, vec_hbm) = refs[:16]
    o_fc2, o_fc1, o_v, o_proj, o_q, o_k, o_layer, o_tok, o_small = refs[16:25]
    rest = refs[25:]
    bufs = [rest[i * BUFFERS : (i + 1) * BUFFERS] for i in range(6)]
    (near, far, far_one, after, mid, low, g_heads, q_s, k_s, v_s, g_proj, wproj, wqkv, n1t, ht, cot, tok, live_s,
     vec, small, small_in, st_fc2, st_fc1, st_qkv,
     free_sem, send_sem, recv_sem, out_sem, away_sem, land_sem, in_sem, st_sem, x_send, x_recv, v_send, v_recv, fin_sem,
     ) = rest[6 * BUFFERS :]
    ins = (g_fc2, g_fc1, None, None, None, None)
    outs = (o_fc2, o_fc1, o_v, o_proj, o_q, o_k)
    stage = (st_fc2, st_fc1, st_qkv, st_fc2, st_qkv, st_qkv)

    me, mp = lax.axis_index("dp"), lax.axis_index("mp")
    core, y, z = me % 2, (me // 2) % 2, me // 4
    to_core = (me + 1 - 2 * core, mp)
    to_y = (me + 2 - 4 * y, mp)
    to_z = (me + 4 - 8 * (z % 2), mp)
    to_mid = (me + 4 - 8 * ((z + 1) % 2), mp)
    to_far = (me + 8 - 16 * (z // 2), mp)
    to_x = (me, 1 - mp)
    centre = z * (3 - z) > 0
    leaf = z * (3 - z) == 0
    upper = z // 2
    tok_rows = near_hbm.shape[0]

    loads = [
        pltpu.make_async_copy(src, dst, in_sem.at[i])
        for i, (src, dst) in enumerate((
            (near_hbm, near), (after_hbm, after), (cot_hbm, cot), (vec_hbm, vec),
            (wproj_hbm, wproj), (q_hbm, q_s), (k_hbm, k_s), (v_hbm, v_s), (live_hbm, live_s), (ht_hbm, ht),
            (n1t_hbm, n1t), (wqkv_hbm, wqkv), (tok_hbm, tok),
        ))
    ]
    for load in loads[:4]:
        load.start()

    barrier = pltpu.get_barrier_semaphore()
    for target in (to_core, to_y, to_z, to_x, to_far):
        pl.semaphore_signal(barrier, inc=1, device_id=target, device_id_type=MESH)

    @pl.when(centre)
    def _():
        pl.semaphore_signal(barrier, inc=1, device_id=to_mid, device_id_type=MESH)
        pl.semaphore_wait(barrier, 6)

    @pl.when(leaf)
    def _():
        pl.semaphore_wait(barrier, 5)

    def copy_x(src, dst, index):
        return pltpu.make_async_remote_copy(
            src_ref=src, dst_ref=dst, send_sem=x_send.at[index], recv_sem=x_recv.at[index],
            device_id=to_x, device_id_type=MESH,
        )

    swap_two = copy_x(near_hbm, far, 0)
    swap_one = copy_x(near, far_one, 1)
    swap_mlp = copy_x(mlp_hbm, far, 2)
    swap_two.start()

    def remote(src, dst, unit, step, target):
        return pltpu.make_async_remote_copy(
            src_ref=src, dst_ref=dst, send_sem=send_sem.at[unit, step], recv_sem=recv_sem.at[unit, step],
            device_id=target, device_id_type=MESH,
        )

    actions = []
    ends = []

    def act(key):
        def keep(fn):
            actions.append((key, len(actions), fn))
            return fn

        return keep

    def both_outputs(src, out, at, size, unit, index):
        place = out.at[rows_at(at, size), :]
        here = pltpu.make_async_copy(src, place, out_sem.at[unit, index])
        there = pltpu.make_async_remote_copy(
            src_ref=src, dst_ref=place, send_sem=away_sem.at[unit, index], recv_sem=land_sem.at[unit, index],
            device_id=to_core, device_id_type=MESH,
        )
        return here, there

    def emit(*args):
        for copy in both_outputs(*args):
            copy.start()

    def product(a, start, size):
        if a == 3:
            return dot_nn(ht[rows_at(start, size), :], low[...])
        return dot_nn(n1t[rows_at(start, size), :], g_proj[{2: 2, 4: 0, 5: 1}[a]])

    unit = 0
    for a, (m, cols, count) in enumerate(layout):
        made = ins[a] is None
        for kind, j in [(kind, j) for j in range(count) for kind in (0, 1)]:
            n, h = m // 2, m // 4
            acc = bufs[a][0].at[kind * count + j]
            y_in, z_in, m_in, rz_in, rm_in, ry_in = (ref.at[j] for ref in bufs[a][1:])
            out = outs[a]
            base = (kind * count + j) * m
            mine, theirs = base + core * n, base + (1 - core) * n
            seq = j * 2 + kind
            t0 = slots[a][j] + (keys["lag"] if kind else 0.0)
            u = unit
            unit += 1
            spare = stage[a].at[seq % 2]
            if not made:
                swap = remote(ins[a].at[rows_at(theirs, n), :], acc, u, 0, to_core)
                load = lambda s, a=a, n=n, m=m, count=count: pltpu.make_async_copy(
                    ins[a].at[rows_at(((s % 2) * count + s // 2) * m + core * n, n), :],
                    stage[a].at[s % 2], st_sem.at[a, s % 2])

                @act(-2.0 + 0.01 * u)
                def _(swap=swap, load=load, seq=seq):
                    swap.start()
                    if seq < 2:
                        load(seq).start()

                def gather(swap=swap, load=load, seq=seq, acc=acc, spare=spare, count=count):
                    load(seq).wait()
                    swap.wait_recv()
                    add_into(acc, acc, spare)
                    if seq + 2 < 2 * count:
                        load(seq + 2).start()
            else:
                swap = remote(spare, acc, u, 0, to_core)

                @act(t0 - keys["ahead"])
                def _(swap=swap, spare=spare, a=a, theirs=theirs, n=n):
                    spare[...] = product(a, theirs, n)
                    swap.start()

                def gather(swap=swap, acc=acc, a=a, mine=mine, n=n):
                    own = product(a, mine, n)
                    swap.wait_recv()
                    acc[...] = acc[...] + own
                    swap.wait_send()

            if kind == 0:
                kept, away = acc.at[rows_at(y * h, h)], acc.at[rows_at((1 - y) * h, h)]
                over = remote(away, y_in, u, 1, to_y)
                up = remote(kept, z_in, u, 2, to_z)
                across = remote(kept, m_in, u, 3, to_mid)
                down = remote(m_in, z_in, u, 4, to_z)
                back_c = remote(m_in, kept, u, 5, to_y)
                back_l = remote(z_in, kept, u, 5, to_y)
                at_kept, at_away = mine + y * h, mine + (1 - y) * h

                @act(t0 + keys["p"][0])
                def _(gather=gather, over=over):
                    gather()
                    over.start()

                @act(t0 + keys["p"][1])
                def _(over=over, up=up, kept=kept, y_in=y_in, u=u):
                    over.wait_recv()
                    add_into(kept, kept, y_in)
                    over.wait_send()
                    pl.semaphore_signal(free_sem.at[u], inc=1, device_id=to_y, device_id_type=MESH)

                    @pl.when(leaf)
                    def _():
                        up.start()

                @act(t0 + keys["p"][2])
                def _(up=up, across=across, kept=kept, z_in=z_in):
                    @pl.when(centre)
                    def _():
                        up.wait_recv()
                        add_into(kept, kept, z_in)
                        across.start()

                @act(t0 + keys["p"][3])
                def _(over=over, across=across, down=down, back_c=back_c, kept=kept, m_in=m_in, out=out,
                      at_kept=at_kept, h=h, u=u):
                    @pl.when(centre)
                    def _():
                        across.wait_recv()
                        add_into(m_in, kept, m_in)
                        down.start()
                        pl.semaphore_wait(free_sem.at[u], 1)
                        back_c.start()
                        emit(m_in, out, at_kept, h, u, 0)

                @act(t0 + keys["p"][4])
                def _(down=down, back_l=back_l, z_in=z_in, out=out, at_kept=at_kept, h=h, u=u):
                    @pl.when(leaf)
                    def _():
                        down.wait_recv()
                        pl.semaphore_wait(free_sem.at[u], 1)
                        back_l.start()
                        emit(z_in, out, at_kept, h, u, 0)

                @act(t0 + keys["p"][5])
                def _(over=over, back_c=back_c, away=away, out=out, at_away=at_away, h=h, u=u):
                    back_c.wait_recv()
                    emit(away, out, at_away, h, u, 1)

                def end(swap=swap, made=made, up=up, across=across, down=down, back_c=back_c, m_in=m_in, away=away,
                        out=out, at_kept=at_kept, at_away=at_away, h=h, u=u):
                    for args in ((m_in, out, at_kept, h, u, 0), (away, out, at_away, h, u, 1)):
                        for copy in both_outputs(*args):
                            copy.wait()
                    if not made:
                        swap.wait_send()
                    back_c.wait_send()

                    @pl.when(leaf)
                    def _():
                        up.wait_send()

                    @pl.when(centre)
                    def _():
                        across.wait_send()
                        down.wait_send()
            else:
                at_own, at_other = upper * h, (1 - upper) * h
                own, other = rows_at(at_own, h), rows_at(at_other, h)
                up = remote(acc, rz_in, u, 1, to_z)
                across = remote(acc.at[other], rm_in, u, 2, to_mid)
                over = remote(acc.at[own], ry_in, u, 3, to_y)
                back = remote(ry_in, acc.at[own], u, 4, to_mid)
                down_a = remote(ry_in, rz_in.at[own], u, 5, to_z)
                down_b = remote(acc.at[other], rz_in.at[other], u, 6, to_z)
                emit_own = (out, mine + at_own, h, u, 0)
                emit_other = (out, mine + at_other, h, u, 1)

                @act(t0 + keys["r"][0])
                def _(gather=gather, up=up):
                    gather()

                    @pl.when(leaf)
                    def _():
                        up.start()

                @act(t0 + keys["r"][1])
                def _(up=up, across=across, acc=acc, rz_in=rz_in):
                    @pl.when(centre)
                    def _():
                        up.wait_recv()
                        add_into(acc, acc, rz_in)
                        across.start()

                @act(t0 + keys["r"][2])
                def _(across=across, over=over, acc=acc, own=own, rm_in=rm_in, u=u):
                    @pl.when(centre)
                    def _():
                        across.wait_recv()
                        add_into(acc.at[own], acc.at[own], rm_in)
                        over.start()
                        across.wait_send()
                        pl.semaphore_signal(free_sem.at[u], inc=1, device_id=to_mid, device_id_type=MESH)

                @act(t0 + keys["r"][3])
                def _(over=over, back=back, down_a=down_a, acc=acc, own=own, ry_in=ry_in, emit_own=emit_own, u=u):
                    @pl.when(centre)
                    def _():
                        over.wait_recv()
                        add_into(ry_in, acc.at[own], ry_in)
                        down_a.start()
                        pl.semaphore_wait(free_sem.at[u], 1)
                        back.start()
                        emit(ry_in, *emit_own)

                @act(t0 + keys["r"][4])
                def _(across=across, back=back, down_b=down_b, acc=acc, other=other, emit_other=emit_other):
                    @pl.when(centre)
                    def _():
                        back.wait_recv()
                        down_b.start()
                        emit(acc.at[other], *emit_other)

                @act(t0 + keys["r"][5])
                def _(down_a=down_a, down_b=down_b, rz_in=rz_in, own=own, other=other, emit_own=emit_own,
                      emit_other=emit_other):
                    @pl.when(leaf)
                    def _():
                        down_a.wait_recv()
                        emit(rz_in.at[own], *emit_own)
                        down_b.wait_recv()
                        emit(rz_in.at[other], *emit_other)

                def end(swap=swap, made=made, up=up, over=over, back=back, down_a=down_a, down_b=down_b, ry_in=ry_in,
                        emit_own=emit_own, emit_other=emit_other):
                    for args in (emit_own, emit_other):
                        for copy in both_outputs(ry_in, *args):
                            copy.wait()
                    if not made:
                        swap.wait_send()

                    @pl.when(leaf)
                    def _():
                        up.wait_send()

                    @pl.when(centre)
                    def _():
                        for copy in (over, back, down_a, down_b):
                            copy.wait_send()

            ends.append(end)

    @act(-1.0)
    def _():
        for load in loads[4:]:
            load.start()

    @act(keys["two"])
    def _():
        for load in loads[:4]:
            load.wait()
        swap_two.wait_recv()
        gain = vec[0:1, :]
        low[pl.ds(tok_rows // 16 * 16, 16), :] = jnp.zeros((16, low.shape[1]), BF16)

        def block(at, carry):
            grad = near[at, :] + far[at, :]
            normal, through = norm_back_rows(after[at, :], grad, gain)
            g_mid = cot[at, :].astype(F32) + through
            mid[at, :] = g_mid
            low[at, :] = g_mid.astype(BF16)
            return tuple(c + fold(v) for c, v in zip(carry, (grad * normal, grad, g_mid)))

        zero = jnp.zeros((1, low.shape[1]), F32)
        sums = each_block(tok_rows, 16, block, (zero, zero, zero))
        small[...] = vec[...]
        for k in range(3):
            small[k + 1 : k + 2, :] = sums[k]

    @act(keys["two"] + 0.001)
    def _():
        loads[4].wait()

        @pl.loop(0, 2)
        def _(i):
            at = pl.ds(pl.multiple_of(i * 256, 256), 256)
            g_heads[at, :] = dot_nt(low[at, :], wproj[...]).astype(BF16)

        for load in loads[5:9]:
            load.wait()

    starts = list(range(0, tok_rows, group))
    lanes = lax.broadcasted_iota(jnp.int32, (1, 128), 1)
    for i, start in enumerate(starts):
        stop = starts[i + 1] if i + 1 < len(starts) else q_s.shape[0]

        @act(keys["attn"][i])
        def _(start=start, size=stop - start):
            rows = pl.ds(start, size)
            first = (lanes < HEAD).astype(F32)

            @pl.loop(0, q_s.shape[1] // 128)
            def _(pair):
                cols = pl.ds(pl.multiple_of(pair * 128, 128), 128)
                live = live_s[rows, pl.ds(0, size)] > 0.0
                grads = attend_back(q_s[rows, cols], k_s[rows, cols], v_s[rows, cols], g_heads[rows, cols], live, first)
                for k in range(3):
                    g_proj[k, rows, cols] = grads[k]

    @act(keys["part"])
    def _():
        for load in loads[9:13]:
            load.wait()
        swap_two.wait_send()

        @pl.loop(0, near.shape[1] // 256)
        def _(i):
            cols = pl.ds(pl.multiple_of(i * 256, 256), 256)
            near[:, cols] = (
                dot_nt(g_proj[0, :tok_rows], wqkv[0, cols, :])
                + dot_nt(g_proj[1, :tok_rows], wqkv[1, cols, :])
                + dot_nt(g_proj[2, :tok_rows], wqkv[2, cols, :])
            )

        swap_one.start()
        zero = jnp.zeros((1, g_proj.shape[2]), F32)
        sums = each_block(
            g_proj.shape[1], 16,
            lambda at, c: tuple(s + fold(g_proj[k, at, :].astype(F32)) for s, k in zip(c, (0, 2))), (zero, zero))
        small[8:9, : g_proj.shape[2]] = sums[0]
        small[8:9, g_proj.shape[2] :] = sums[1]

    own_mlp = pltpu.make_async_copy(mlp_hbm, near, in_sem.at[0])
    put_tok = pltpu.make_async_copy(cot, o_tok, fin_sem.at[0])
    put_layer = pltpu.make_async_copy(tok, o_layer, fin_sem.at[1])

    @act(keys["one"])
    def _():
        swap_one.wait_recv()
        swap_mlp.start()
        gain = vec[9:10, :]

        def block(at, carry):
            grad = near[at, :] + far_one[at, :]
            normal, through = norm_back_rows(tok[at, :].astype(F32), grad, gain)
            cot[at, :] = (mid[at, :] + through).astype(BF16)
            return tuple(c + fold(v) for c, v in zip(carry, (grad * normal, grad)))

        zero = jnp.zeros((1, near.shape[1]), F32)
        sums = each_block(tok_rows, 16, block, (zero, zero))
        for k in range(2):
            small[k + 4 : k + 5, :] = sums[k]
        put_tok.start()
        swap_one.wait_send()
        own_mlp.start()

    @act(keys["layer"])
    def _():
        own_mlp.wait()
        swap_mlp.wait_recv()
        shift = vec[10:11, :]

        def block(at, carry):
            tok[at, :] = (after[at, :] + (near[at, :] + far[at, :]) + shift).astype(BF16)
            return carry

        each_block(tok_rows, 16, block)
        put_layer.start()

    doubles = [
        pltpu.make_async_remote_copy(
            src_ref=small, dst_ref=small_in.at[k], send_sem=v_send.at[k], recv_sem=v_recv.at[k],
            device_id=target, device_id_type=MESH,
        )
        for k, target in enumerate((to_core, to_y, to_z, to_far))
    ]
    for k in range(5):
        @act(keys["small"][k])
        def _(k=k):
            if k:
                doubles[k - 1].wait()
                small[...] = small[...] + small_in[k - 1]
            if k < 4:
                doubles[k].start()
            else:
                put_small.start()

    put_small = pltpu.make_async_copy(small, o_small, fin_sem.at[2])

    for _, _, fn in sorted(actions, key=lambda t: t[:2]):
        fn()
    swap_mlp.wait_send()
    for copy in (put_tok, put_layer, put_small):
        copy.wait()
    for end in ends:
        end()


KEYS = {
    "lag": 0.4, "ahead": 0.8,
    "p": (0, 2.0, 3.5, 5.0, 6.5, 8.0), "r": (0, 2.0, 3.3, 4.7, 6.0, 8.0),
    "two": 3.0, "attn": (3.3, 3.6, 3.9), "part": 4.2, "one": 8.0, "layer": 10.6,
    "small": (9.0, 9.5, 10.0, 10.5, 11.0),
}


def backward(args, group, keys=KEYS):
    g_fc2, g_fc1 = args[0], args[1]
    tok_rows, width = args[2].shape
    cols = args[7].shape[1]
    pad_rows = args[7].shape[0]
    shapes = [g_fc2.shape, g_fc1.shape, (width, cols), (cols, width), (width, cols), (width, cols)]
    layout = split_plan(shapes)
    slots, at = [], 0.0
    for m, c, count in layout:
        slots.append([at + j for j in range(count)])
        at += count
    scratch, units = [], 0
    for m, c, count in layout:
        units += 2 * count
        n, h = m // 2, m // 4
        for lead, rows in ((2 * count, n), (count, h), (count, h), (count, h), (count, n), (count, h), (count, h)):
            scratch.append(pltpu.VMEM((lead, rows, c), F32))
    dma = pltpu.SemaphoreType.DMA
    scratch += [
        pltpu.VMEM((tok_rows, width), F32), pltpu.VMEM((tok_rows, width), F32), pltpu.VMEM((tok_rows, width), F32),
        pltpu.VMEM((tok_rows, width), F32), pltpu.VMEM((tok_rows, width), F32), pltpu.VMEM((pad_rows, width), BF16),
        pltpu.VMEM((pad_rows, cols), BF16), pltpu.VMEM((pad_rows, cols), BF16), pltpu.VMEM((pad_rows, cols), BF16),
        pltpu.VMEM((pad_rows, cols), BF16), pltpu.VMEM((3, pad_rows, cols), BF16), pltpu.VMEM((cols, width), BF16),
        pltpu.VMEM((3, width, cols), BF16), pltpu.VMEM((width, pad_rows), BF16), pltpu.VMEM((cols, pad_rows), BF16),
        pltpu.VMEM((tok_rows, width), BF16), pltpu.VMEM((tok_rows, width), BF16), pltpu.VMEM(args[10].shape, F32),
        pltpu.VMEM((16, width), F32), pltpu.VMEM((16, width), F32), pltpu.VMEM((4, 16, width), F32),
        pltpu.VMEM((2, layout[0][0] // 2, layout[0][1]), F32), pltpu.VMEM((2, layout[1][0] // 2, layout[1][1]), F32),
        pltpu.VMEM((2, layout[2][0] // 2, layout[2][1]), F32),
        pltpu.SemaphoreType.REGULAR((units,)), dma((units, 7)), dma((units, 7)), dma((units, 2)), dma((units, 2)), dma((units, 2)),
        dma((13,)), dma((2, 2)), dma((3,)), dma((3,)), dma((4,)), dma((4,)), dma((3,)),
    ]
    spec = pl.BlockSpec(memory_space=pl.ANY)
    shape = jax.ShapeDtypeStruct
    return pl.pallas_call(
        functools.partial(back_kernel, layout, keys, slots, group),
        out_shape=[shape(s, F32) for s in shapes]
        + [shape((tok_rows, width), BF16), shape((tok_rows, width), BF16), shape((16, width), F32)],
        in_specs=[spec] * 16,
        out_specs=[spec] * 9,
        scratch_shapes=scratch,
        name="backward",
        compiler_params=pltpu.CompilerParams(
            collective_id=0, has_side_effects=True, vmem_limit_bytes=67043328
        ),
    )(*args)


def make_body(n_dp, n_mp):
    fast = n_dp == 16 and n_mp == 2

    def sum_mp(part):
        if n_mp == 2:
            return part + swap(part, "mp", 2, 1)
        return lax.psum(part, "mp")

    def body(
        tokens, keep_mask, ln1_gain, ln1_bias, w_qkv, b_qkv, w_proj, b_proj,
        ln2_gain, ln2_bias, w_fc1, b_fc1, w_fc2, b_fc2, cotangent,
    ):
        inputs = tokens.astype(F32)
        tok_rows, width = inputs.shape
        images = keep_mask.shape[0]
        slots = tok_rows // images
        cols = w_qkv.shape[2]
        heads = cols // HEAD
        shape = (images, slots, heads, HEAD)

        normal_one, inverse_one = norm_parts(inputs)
        norm_one = (normal_one * ln1_gain + ln1_bias).astype(BF16)
        weight = w_qkv.transpose(1, 0, 2)
        query = (dot_nn(norm_one, weight[0]) + b_qkv[0]).astype(BF16).reshape(shape)
        keys = dot_nn(norm_one, weight[1]).astype(BF16).reshape(shape)
        values = (dot_nn(norm_one, weight[2]) + b_qkv[1]).astype(BF16).reshape(shape)
        scores = jnp.einsum("bqhd,bkhd->bhqk", query, keys, preferred_element_type=F32) * 0.125
        live = (keep_mask > 0)[:, None, None, :]
        masked = jnp.where(live, scores, -1e30)
        row_max = jnp.max(masked, axis=-1, keepdims=True)
        exp_terms = jnp.where(live, jnp.exp(masked - row_max), 0.0)
        probs = exp_terms / jnp.sum(exp_terms, axis=-1, keepdims=True)
        probs_low = probs.astype(BF16)
        mixed = jnp.einsum("bhqk,bkhd->bqhd", probs_low, values, preferred_element_type=F32)
        heads_out = mixed.reshape(tok_rows, cols).astype(BF16)
        after_attn = inputs + sum_mp(dot_nn(heads_out, w_proj)) + b_proj

        normal_two, inverse_two = norm_parts(after_attn)
        norm_two = (normal_two * ln2_gain + ln2_bias).astype(BF16)
        pre_act = dot_nn(norm_two, w_fc1) + b_fc1
        hidden_f, gelu_back = jax.vjp(lambda v: jax.nn.gelu(v, approximate=False), pre_act)
        hidden = hidden_f.astype(BF16)
        grad_w_fc2 = dot_tn(hidden, cotangent)
        grad_pre = gelu_back(dot_nt(cotangent, w_fc2))[0].astype(BF16)
        norm_two_part = dot_nt(grad_pre, w_fc1)
        grad_w_fc1 = dot_tn(norm_two, grad_pre)
        mlp_part = dot_nn(hidden, w_fc2)
        grad_out = cotangent.astype(F32)
        sum_out = jnp.sum(grad_out, axis=0)
        sum_pre = jnp.sum(grad_pre.astype(F32), axis=0)
        if fast:
            pad = -tok_rows % 128
            group = 4 * slots
            image = jnp.arange(tok_rows + pad) // slots
            place = jnp.arange(256)
            base = jnp.arange(tok_rows + pad) // group * 4
            key_image = base[:, None] + place[None, :] // slots
            kept = jnp.pad(keep_mask, ((0, 2), (0, 0)))
            rows_kept = jnp.concatenate(
                [
                    jnp.broadcast_to(kept[4 * g : 4 * g + 4].reshape(1, group), (size, group))
                    for g, size in enumerate((group, group, tok_rows + pad - 2 * group))
                ]
            )
            rows_kept = jnp.pad(rows_kept, ((0, 0), (0, 256 - group)))
            live_map = ((image[:, None] == key_image) & (rows_kept > 0)).astype(F32)
            vec = jnp.concatenate(
                [
                    ln2_gain,
                    jnp.zeros(5 * width, F32),
                    sum_pre,
                    jnp.zeros(width, F32),
                    ln1_gain,
                    b_fc2,
                    sum_out,
                    jnp.zeros(4 * width, F32),
                ]
            ).reshape(16, width)
            padded = lambda v: jnp.pad(v.reshape(tok_rows, -1), ((0, pad), (0, 0)))
            results = backward(
                (
                    grad_w_fc2,
                    grad_w_fc1,
                    norm_two_part,
                    mlp_part,
                    after_attn,
                    tokens,
                    cotangent,
                    padded(query),
                    padded(keys),
                    padded(values),
                    live_map,
                    w_proj,
                    weight,
                    padded(norm_one).T,
                    padded(heads_out).T,
                    vec,
                ),
                group,
            )
            grad_w_fc2, grad_w_fc1, grad_w_v, grad_w_proj, grad_w_q, grad_w_k = results[:6]
            layer_out, grad_tokens, small = results[6:]
            return (
                layer_out,
                grad_tokens,
                small[4],
                small[5],
                jnp.stack([grad_w_q, grad_w_k, grad_w_v], axis=1),
                small[8].reshape(2, cols),
                grad_w_proj,
                small[3],
                small[1],
                small[2],
                grad_w_fc1,
                small[6:8].reshape(-1),
                grad_w_fc2,
                small[11],
            )

        grad_norm_two = sum_mp(norm_two_part)
        layer_out = (after_attn + sum_mp(mlp_part) + b_fc2).astype(BF16)
        grad_mid = grad_out + norm_back(grad_norm_two, normal_two, inverse_two, ln2_gain)
        grad_mid_low = grad_mid.astype(BF16)
        grad_heads = dot_nt(grad_mid_low, w_proj).astype(BF16).reshape(shape)
        grad_w_proj = dot_tn(heads_out, grad_mid_low)
        grad_probs = jnp.einsum("bqhd,bkhd->bhqk", grad_heads, values, preferred_element_type=F32)
        grad_values = jnp.einsum(
            "bhqk,bqhd->bkhd", probs_low, grad_heads, preferred_element_type=F32
        ).astype(BF16)
        inner = jnp.sum(probs * grad_probs, axis=-1, keepdims=True)
        grad_scores = (probs * (grad_probs - inner)).astype(BF16)
        grad_query = (
            jnp.einsum("bhqk,bkhd->bqhd", grad_scores, keys, preferred_element_type=F32) * 0.125
        ).astype(BF16)
        grad_keys = (
            jnp.einsum("bhqk,bqhd->bkhd", grad_scores, query, preferred_element_type=F32) * 0.125
        ).astype(BF16)
        grad_query = grad_query.reshape(tok_rows, cols)
        grad_keys = grad_keys.reshape(tok_rows, cols)
        grad_values = grad_values.reshape(tok_rows, cols)
        part = (
            dot_nt(grad_query, weight[0])
            + dot_nt(grad_keys, weight[1])
            + dot_nt(grad_values, weight[2])
        )
        grad_norm_one = sum_mp(part)
        grads = [
            grad_w_fc2,
            grad_w_fc1,
            grad_w_proj,
            dot_tn(norm_one, grad_values),
            dot_tn(norm_one, grad_query),
            dot_tn(norm_one, grad_keys),
        ]
        grads = lax.psum(grads, "dp")
        grad_w_fc2, grad_w_fc1, grad_w_proj, grad_w_v, grad_w_q, grad_w_k = grads
        grad_w_qkv = jnp.stack([grad_w_q, grad_w_k, grad_w_v], axis=1)
        grad_tokens = (
            grad_mid + norm_back(grad_norm_one, normal_one, inverse_one, ln1_gain)
        ).astype(BF16)

        small = jnp.concatenate(
            [
                sum_out,
                jnp.sum(grad_norm_two * normal_two, axis=0),
                jnp.sum(grad_norm_two, axis=0),
                jnp.sum(grad_mid, axis=0),
                jnp.sum(grad_norm_one * normal_one, axis=0),
                jnp.sum(grad_norm_one, axis=0),
                sum_pre,
                jnp.sum(grad_query.astype(F32), axis=0),
                jnp.sum(grad_values.astype(F32), axis=0),
            ]
        )
        small = lax.psum(small, "dp")
        rows = [small[k * width : (k + 1) * width] for k in range(6)]
        spot = 6 * width + b_fc1.shape[0]
        return (
            layer_out,
            grad_tokens,
            rows[4],
            rows[5],
            grad_w_qkv,
            small[spot:].reshape(2, cols),
            grad_w_proj,
            rows[3],
            rows[1],
            rows[2],
            grad_w_fc1,
            small[6 * width : spot],
            grad_w_fc2,
            rows[0],
        )

    return body


def solution(mesh):
    return jax.shard_map(
        make_body(mesh.shape["dp"], mesh.shape["mp"]),
        mesh=mesh,
        in_specs=(
            P("dp", None),
            P("dp", None),
            P(),
            P(),
            P(None, None, "mp"),
            P(None, "mp"),
            P("mp", None),
            P(),
            P(),
            P(),
            P(None, "mp"),
            P("mp"),
            P("mp", None),
            P(),
            P("dp", None),
        ),
        out_specs=(
            P("dp", None),
            P("dp", None),
            P(),
            P(),
            P(None, None, "mp"),
            P(None, "mp"),
            P("mp", None),
            P(),
            P(),
            P(),
            P(None, "mp"),
            P("mp"),
            P("mp", None),
            P(),
        ),
        check_vma=False,
    )
```

```python
import functools

import jax
import jax.numpy as jnp
from jax import lax
from jax.experimental import pallas as pl
from jax.experimental.pallas import tpu as pltpu
from jax.sharding import PartitionSpec as P

HEAD = 64
BF16 = jnp.bfloat16
MESH = pl.DeviceIdType.MESH
F32 = jnp.float32


def dot_nn(left, right):
    return jnp.dot(left, right, preferred_element_type=F32)


def dot_tn(left, right):
    return lax.dot_general(left, right, (((0,), (0,)), ((), ())), preferred_element_type=F32)


def dot_nt(left, right):
    return lax.dot_general(left, right, (((1,), (1,)), ((), ())), preferred_element_type=F32)


def norm_parts(value):
    centered = value - jnp.mean(value, axis=-1, keepdims=True)
    variance = jnp.mean(centered * centered, axis=-1, keepdims=True)
    inverse = lax.rsqrt(variance + 1e-06)
    return centered * inverse, inverse


def norm_back(grad, normalized, inverse, gain):
    scaled = grad * gain
    mean_one = jnp.mean(scaled, axis=-1, keepdims=True)
    mean_two = jnp.mean(scaled * normalized, axis=-1, keepdims=True)
    return inverse * (scaled - mean_one - normalized * mean_two)


def swap(value, axis, size, mask):
    return lax.ppermute(value, axis, [(i, i ^ mask) for i in range(size)])


def split_plan(shapes, unit_bytes=1 << 20):
    out = []
    for rows, cols in shapes:
        count = max(1, rows * cols * 4 // 2 // unit_bytes)
        out.append((rows // 2 // count, cols, count))
    return out


def rows_at(start, size):
    return pl.ds(pl.multiple_of(start, 8), size)


def each_block(total, step, body, carry=()):
    full = total // step
    if full:
        carry = lax.fori_loop(
            0, full, lambda i, c: body(pl.ds(pl.multiple_of(i * step, step), step), c), carry
        )
    if total % step:
        carry = body(pl.ds(full * step, total % step), carry)
    return carry


def add_into(dst, src_a, src_b):
    @pl.loop(0, dst.shape[0] // 16)
    def _(i):
        at = pl.ds(pl.multiple_of(i * 16, 16), 16)
        dst[at, :] = src_a[at, :] + src_b[at, :]


def fold(value):
    return jnp.sum(value, axis=0, keepdims=True)


def norm_back_rows(value, grad, gain):
    normal, inverse = norm_parts(value)
    return normal, norm_back(grad, normal, inverse, gain)


def attend_back(q, k, v, g, live, first):
    grad_q = grad_k = grad_v = None
    for own in (first, 1 - first):
        own = own.astype(BF16)
        q_own, g_own, k_own = q * own, g * own, k * own
        scores = jnp.where(live, dot_nt(q_own, k) * 0.125, -1e30)
        exp_terms = jnp.where(live, jnp.exp(scores - jnp.max(scores, axis=-1, keepdims=True)), 0.0)
        probs = exp_terms / jnp.maximum(jnp.sum(exp_terms, axis=-1, keepdims=True), 1.0)
        grad_probs = dot_nt(g_own, v)
        inner = jnp.sum(probs * grad_probs, axis=-1, keepdims=True)
        grad_scores = (probs * (grad_probs - inner)).astype(BF16)
        parts = (dot_nn(grad_scores, k_own), dot_tn(grad_scores, q_own), dot_tn(probs.astype(BF16), g_own))
        if grad_q is None:
            grad_q, grad_k, grad_v = parts
        else:
            grad_q, grad_k, grad_v = grad_q + parts[0], grad_k + parts[1], grad_v + parts[2]
    return (grad_q * 0.125).astype(BF16), (grad_k * 0.125).astype(BF16), grad_v.astype(BF16)


def attend(q, k, v, live, first):
    mixed = None
    for own in (first, 1 - first):
        own = own.astype(BF16)
        scores = jnp.where(live, dot_nt(q * own, k) * 0.125, -1e30)
        exp_terms = jnp.where(live, jnp.exp(scores - jnp.max(scores, axis=-1, keepdims=True)), 0.0)
        probs = exp_terms / jnp.maximum(jnp.sum(exp_terms, axis=-1, keepdims=True), 1.0)
        part = dot_nn(probs.astype(BF16), v * own)
        mixed = part if mixed is None else mixed + part
    return mixed


def groups_of(tok_rows, pad_rows, group):
    starts = list(range(0, tok_rows, group))
    return [(a, b - a) for a, b in zip(starts, starts[1:] + [pad_rows])]


def front_kernel(slots, group, *refs):
    (tok_hbm, kept_hbm, wqkv_hbm, wproj_hbm, wfc1_hbm, wfc2_hbm, cot_hbm, vec_hbm) = refs[:8]
    outs = refs[8:21]
    (tok, kept, wqkv, wproj, wfc1, wfc2, cot, vec,
     n1, q_s, k_s, v_s, heads, live_s, after, n2, hidden, g_pre, near, mlp,
     h_all, w_all, w_wide, w_got, h_send, h_got,
     in_sem, out_sem, w_send, w_recv, g_send, g_recv) = refs[21:]
    me, mp = lax.axis_index("dp"), lax.axis_index("mp")
    core, y = me % 2, (me // 2) % 2
    to_core = (me + 1 - 2 * core, mp)
    to_y = (me + 2 - 4 * y, mp)
    to_x = (me, 1 - mp)
    tok_rows, width = tok.shape
    pad_rows, cols = q_s.shape
    quarter = w_wide.shape[0]

    loads = [
        pltpu.make_async_copy(src, dst, in_sem.at[i])
        for i, (src, dst) in enumerate((
            (wproj_hbm, wproj), (tok_hbm, tok), (vec_hbm, vec), (kept_hbm, kept), (wqkv_hbm, wqkv),
            (wfc1_hbm, wfc1), (wfc2_hbm, wfc2), (cot_hbm, cot),
        ))
    ]
    for load in loads:
        load.start()
    barrier = pltpu.get_barrier_semaphore()
    for target in (to_core, to_y, to_x):
        pl.semaphore_signal(barrier, inc=1, device_id=target, device_id_type=MESH)

    def remote(src, dst, send, recv, index, target):
        return pltpu.make_async_remote_copy(
            src_ref=src, dst_ref=dst, send_sem=send.at[index], recv_sem=recv.at[index],
            device_id=target, device_id_type=MESH,
        )

    place = core * 2 + y
    w_steps = (
        remote(w_wide, w_got.at[place], w_send, w_recv, 0, to_x),
        remote(w_got.at[place], w_got.at[place], w_send, w_recv, 1, to_y),
        remote(w_got.at[pl.ds(core * 2, 2)], w_got.at[pl.ds(core * 2, 2)], w_send, w_recv, 2, to_core),
    )
    loads[0].wait()
    w_wide[...] = wproj[rows_at(place * quarter, quarter), :].astype(F32)
    pl.semaphore_wait(barrier, 3)
    w_steps[0].start()

    for load in loads[1:3]:
        load.wait()
    n1[pl.ds(tok_rows // 16 * 16, 16), :] = jnp.zeros((16, width), BF16)
    n2[pl.ds(tok_rows // 16 * 16, 16), :] = jnp.zeros((16, width), BF16)

    def norm_block(src, dst, gain, shift):
        def block(at, carry):
            normal, _ = norm_parts(src[at, :].astype(F32))
            dst[at, :] = (normal * gain + shift).astype(BF16)
            return carry

        each_block(tok_rows, 16, block)

    norm_block(tok, n1, vec[9:10, :], vec[3:4, :])
    loads[4].wait()
    for i, dst in enumerate((q_s, k_s, v_s)):
        @pl.loop(0, cols // 256)
        def _(t):
            at = pl.ds(pl.multiple_of(t * 256, 256), 256)
            value = dot_nn(n1[...], wqkv[i, :, at])
            if i != 1:
                value = value + vec[4:5, pl.ds(pl.multiple_of(t * 256 + i // 2 * cols, 256), 256)]
            dst[:, at] = value.astype(BF16)

    w_steps[0].wait_recv()
    w_steps[1].start()
    loads[3].wait()
    lanes = lax.broadcasted_iota(jnp.int32, (1, 128), 1)
    first = (lanes < HEAD).astype(F32)
    live_s[...] = jnp.zeros_like(live_s)
    sends = []
    for g, (start, size) in enumerate(groups_of(tok_rows, pad_rows, group)):
        rows = pl.ds(start, size)
        row = lax.broadcasted_iota(jnp.int32, (size, size), 0)
        col = lax.broadcasted_iota(jnp.int32, (size, size), 1)
        image_of = lambda v: sum((v >= slots * (k + 1)).astype(jnp.int32) for k in range(group // slots - 1))
        same = (image_of(row) == image_of(col)).astype(F32)
        live_s[rows, pl.ds(0, size)] = same * kept[g : g + 1, pl.ds(0, size)]

        @pl.loop(0, cols // 128)
        def _(pair):
            at = pl.ds(pl.multiple_of(pair * 128, 128), 128)
            live = live_s[rows, pl.ds(0, size)] > 0.0
            mixed = attend(q_s[rows, at], k_s[rows, at], v_s[rows, at], live, first).astype(BF16)
            heads[rows, at] = mixed
            h_send[rows, at] = mixed.astype(F32)

        send = remote(h_send.at[rows], h_got.at[rows], g_send, g_recv, g, to_x)
        send.start()
        sends.append(send)
        if g == 0:
            w_steps[1].wait_recv()
            w_steps[2].start()

    puts = []

    def put(src, index):
        copy = pltpu.make_async_copy(src, outs[index], out_sem.at[index])
        copy.start()
        puts.append(copy)

    for index, src in enumerate((n1, q_s, k_s, v_s, heads, live_s)):
        put(src, index)
    mine, other = pl.ds(pl.multiple_of(mp * cols, 128), cols), pl.ds(pl.multiple_of((1 - mp) * cols, 128), cols)
    h_all[:, mine] = heads[...]
    w_all[mine, :] = wproj[...]
    loads[7].wait()
    total = each_block(
        tok_rows, 16, lambda at, c: c + fold(cot[at, :].astype(F32)), jnp.zeros((1, width), F32)
    )
    w_steps[2].wait_recv()
    for k in range(4):
        w_all[pl.ds(pl.multiple_of((1 - mp) * cols + k * quarter, 128), quarter), :] = w_got[k].astype(BF16)
    for send, (start, size) in zip(sends, groups_of(tok_rows, pad_rows, group)):
        rows = pl.ds(start, size)
        send.wait_recv()
        h_all[rows, other] = h_got[rows, :].astype(BF16)

    @pl.loop(0, width // 256)
    def _(t):
        at = pl.ds(pl.multiple_of(t * 256, 256), 256)
        after[:, at] = (
            tok[:, at].astype(F32) + dot_nn(h_all[:tok_rows, :], w_all[:, at]) + vec[2:3, at]
        )

    put(after, 6)
    norm_block(after, n2, vec[0:1, :], vec[1:2, :])
    put(n2, 7)
    loads[5].wait()
    loads[6].wait()
    hidden[pl.ds(tok_rows // 16 * 16, 16), :] = jnp.zeros((16, hidden.shape[1]), BF16)
    g_pre[pl.ds(tok_rows // 16 * 16, 16), :] = jnp.zeros((16, hidden.shape[1]), BF16)
    per_row = width // 256

    @pl.loop(0, hidden.shape[1] // 256)
    def _(t):
        at = pl.ds(pl.multiple_of(t * 256, 256), 256)
        bias_row = 6 + t // per_row
        bias_at = pl.ds(pl.multiple_of(t % per_row * 256, 256), 256)
        bias = vec[pl.ds(bias_row, 1), bias_at]
        sums = jnp.zeros((1, 256), F32)
        for start in range(0, tok_rows, 256):
            rows = pl.ds(start, min(256, tok_rows - start))
            pre = dot_nn(n2[rows, :], wfc1[:, at]) + bias
            cdf = 0.5 * (1.0 + lax.erf(pre * 0.7071067811865476))
            hidden[rows, at] = (pre * cdf).astype(BF16)
            slope = cdf + pre * (jnp.exp(pre * pre * -0.5) * 0.3989422804014327)
            grad = (dot_nt(cot[rows, :], wfc2[at, :]) * slope).astype(BF16)
            g_pre[rows, at] = grad
            sums = sums + fold(grad.astype(F32))
        vec[pl.ds(bias_row, 1), bias_at] = sums

    vec[11:12, :] = total
    put(vec, 12)
    put(g_pre, 9)
    put(hidden, 8)

    @pl.loop(0, width // 256)
    def _(t):
        at = pl.ds(pl.multiple_of(t * 256, 256), 256)
        near[:, at] = dot_nt(g_pre[:tok_rows, :], wfc1[at, :])
        mlp[:, at] = dot_nn(hidden[:tok_rows, :], wfc2[:, at])

    put(near, 10)
    put(mlp, 11)
    for copy in w_steps:
        copy.wait_send()
    for send in sends:
        send.wait_send()
    for copy in puts:
        copy.wait()


def front(args, slots, group, hidden_cols):
    tok_rows, width = args[0].shape
    cols = args[3].shape[0]
    pad_rows = tok_rows + -tok_rows % 128
    low = [(pad_rows, width)] + [(pad_rows, cols)] * 4
    outs = (
        [(s, BF16) for s in low]
        + [((pad_rows, 256), F32), ((tok_rows, width), F32), ((pad_rows, width), BF16)]
        + [((pad_rows, hidden_cols), BF16)] * 2
        + [((tok_rows, width), F32)] * 2
        + [((16, width), F32)]
    )
    quarter = cols // 4
    dma = pltpu.SemaphoreType.DMA
    scratch = [pltpu.VMEM(a.shape, a.dtype) for a in args]
    scratch += [pltpu.VMEM(s, d) for s, d in outs[:-1]]
    scratch += [
        pltpu.VMEM((pad_rows, 2 * cols), BF16), pltpu.VMEM((2 * cols, width), BF16),
        pltpu.VMEM((quarter, width), F32), pltpu.VMEM((4, quarter, width), F32),
        pltpu.VMEM((pad_rows, cols), F32), pltpu.VMEM((pad_rows, cols), F32),
        dma((8,)), dma((13,)), dma((3,)), dma((3,)), dma((3,)), dma((3,)),
    ]
    spec = pl.BlockSpec(memory_space=pl.ANY)
    return pl.pallas_call(
        functools.partial(front_kernel, slots, group),
        out_shape=[jax.ShapeDtypeStruct(s, d) for s, d in outs],
        in_specs=[spec] * 8,
        out_specs=[spec] * 13,
        scratch_shapes=scratch,
        name="front",
        compiler_params=pltpu.CompilerParams(
            collective_id=1, has_side_effects=True, vmem_limit_bytes=62 << 20
        ),
    )(*args)


BUFFERS = 7


def back_kernel(layout, keys, slots, group, *refs):
    (g_fc2, g_fc1, near_hbm, mlp_hbm, after_hbm, tok_hbm, cot_hbm, q_hbm, k_hbm, v_hbm, live_hbm, wproj_hbm,
     wqkv_hbm, n1_hbm, heads_hbm, vec_hbm) = refs[:16]
    o_fc2, o_fc1, o_v, o_proj, o_q, o_k, o_layer, o_tok, o_small = refs[16:25]
    rest = refs[25:]
    bufs = [rest[i * BUFFERS : (i + 1) * BUFFERS] for i in range(6)]
    (near, far, far_one, after, mid, low, g_heads, q_s, k_s, v_s, g_proj, wproj, wqkv, n1, heads, cot, tok, live_s,
     vec, small, small_in, st_fc2, st_fc1, st_qkv,
     free_sem, send_sem, recv_sem, out_sem, away_sem, land_sem, in_sem, st_sem, x_send, x_recv, v_send, v_recv, fin_sem,
     ) = rest[6 * BUFFERS :]
    ins = (g_fc2, g_fc1, None, None, None, None)
    outs = (o_fc2, o_fc1, o_v, o_proj, o_q, o_k)
    stage = (st_fc2, st_fc1, st_qkv, st_fc2, st_qkv, st_qkv)

    me, mp = lax.axis_index("dp"), lax.axis_index("mp")
    core, y, z = me % 2, (me // 2) % 2, me // 4
    to_core = (me + 1 - 2 * core, mp)
    to_y = (me + 2 - 4 * y, mp)
    to_z = (me + 4 - 8 * (z % 2), mp)
    to_mid = (me + 4 - 8 * ((z + 1) % 2), mp)
    to_far = (me + 8 - 16 * (z // 2), mp)
    to_x = (me, 1 - mp)
    centre = z * (3 - z) > 0
    leaf = z * (3 - z) == 0
    upper = z // 2
    tok_rows = near_hbm.shape[0]

    loads = [
        pltpu.make_async_copy(src, dst, in_sem.at[i])
        for i, (src, dst) in enumerate((
            (near_hbm, near), (after_hbm, after), (cot_hbm, cot), (vec_hbm, vec),
            (wproj_hbm, wproj), (q_hbm, q_s), (k_hbm, k_s), (v_hbm, v_s), (live_hbm, live_s), (heads_hbm, heads),
            (n1_hbm, n1), (wqkv_hbm, wqkv), (tok_hbm, tok),
        ))
    ]
    for load in loads[:4]:
        load.start()

    barrier = pltpu.get_barrier_semaphore()
    for target in (to_core, to_y, to_z, to_x, to_far):
        pl.semaphore_signal(barrier, inc=1, device_id=target, device_id_type=MESH)

    @pl.when(centre)
    def _():
        pl.semaphore_signal(barrier, inc=1, device_id=to_mid, device_id_type=MESH)
        pl.semaphore_wait(barrier, 6)

    @pl.when(leaf)
    def _():
        pl.semaphore_wait(barrier, 5)

    def copy_x(src, dst, index):
        return pltpu.make_async_remote_copy(
            src_ref=src, dst_ref=dst, send_sem=x_send.at[index], recv_sem=x_recv.at[index],
            device_id=to_x, device_id_type=MESH,
        )

    swap_two = copy_x(near_hbm, far, 0)
    swap_one = copy_x(near, far_one, 1)
    swap_mlp = copy_x(mlp_hbm, far, 2)
    swap_two.start()

    def remote(src, dst, unit, step, target):
        return pltpu.make_async_remote_copy(
            src_ref=src, dst_ref=dst, send_sem=send_sem.at[unit, step], recv_sem=recv_sem.at[unit, step],
            device_id=target, device_id_type=MESH,
        )

    actions = []
    ends = []

    def act(key):
        def keep(fn):
            actions.append((key, len(actions), fn))
            return fn

        return keep

    def both_outputs(src, out, at, size, unit, index):
        place = out.at[rows_at(at, size), :]
        here = pltpu.make_async_copy(src, place, out_sem.at[unit, index])
        there = pltpu.make_async_remote_copy(
            src_ref=src, dst_ref=place, send_sem=away_sem.at[unit, index], recv_sem=land_sem.at[unit, index],
            device_id=to_core, device_id_type=MESH,
        )
        return here, there

    def emit(*args):
        for copy in both_outputs(*args):
            copy.start()

    def product(a, start, size):
        if a == 3:
            return dot_tn(heads[:, pl.ds(pl.multiple_of(start, 128), size)], low[...])
        return dot_tn(n1[:, pl.ds(pl.multiple_of(start, 128), size)], g_proj[{2: 2, 4: 0, 5: 1}[a]])

    unit = 0
    for a, (m, cols, count) in enumerate(layout):
        made = ins[a] is None
        for kind, j in [(kind, j) for j in range(count) for kind in (0, 1)]:
            n, h = m // 2, m // 4
            acc = bufs[a][0].at[kind * count + j]
            y_in, z_in, m_in, rz_in, rm_in, ry_in = (ref.at[j] for ref in bufs[a][1:])
            out = outs[a]
            base = (kind * count + j) * m
            mine, theirs = base + core * n, base + (1 - core) * n
            seq = j * 2 + kind
            t0 = slots[a][j] + (keys["lag"] if kind else 0.0)
            u = unit
            unit += 1
            spare = stage[a].at[seq % 2]
            if not made:
                swap = remote(ins[a].at[rows_at(theirs, n), :], acc, u, 0, to_core)
                load = lambda s, a=a, n=n, m=m, count=count: pltpu.make_async_copy(
                    ins[a].at[rows_at(((s % 2) * count + s // 2) * m + core * n, n), :],
                    stage[a].at[s % 2], st_sem.at[a, s % 2])

                @act(-2.0 + 0.01 * u)
                def _(swap=swap, load=load, seq=seq):
                    swap.start()
                    if seq < 2:
                        load(seq).start()

                def gather(swap=swap, load=load, seq=seq, acc=acc, spare=spare, count=count):
                    load(seq).wait()
                    swap.wait_recv()
                    add_into(acc, acc, spare)
                    if seq + 2 < 2 * count:
                        load(seq + 2).start()
            else:
                swap = remote(spare, acc, u, 0, to_core)

                @act(t0 - keys["ahead"])
                def _(swap=swap, spare=spare, a=a, theirs=theirs, n=n):
                    spare[...] = product(a, theirs, n)
                    swap.start()

                def gather(swap=swap, acc=acc, a=a, mine=mine, n=n):
                    own = product(a, mine, n)
                    swap.wait_recv()
                    acc[...] = acc[...] + own
                    swap.wait_send()

            if kind == 0:
                kept, away = acc.at[rows_at(y * h, h)], acc.at[rows_at((1 - y) * h, h)]
                over = remote(away, y_in, u, 1, to_y)
                up = remote(kept, z_in, u, 2, to_z)
                across = remote(kept, m_in, u, 3, to_mid)
                down = remote(m_in, z_in, u, 4, to_z)
                back_c = remote(m_in, kept, u, 5, to_y)
                back_l = remote(z_in, kept, u, 5, to_y)
                at_kept, at_away = mine + y * h, mine + (1 - y) * h

                @act(t0 + keys["p"][0])
                def _(gather=gather, over=over):
                    gather()
                    over.start()

                @act(t0 + keys["p"][1])
                def _(over=over, up=up, kept=kept, y_in=y_in, u=u):
                    over.wait_recv()
                    add_into(kept, kept, y_in)
                    over.wait_send()
                    pl.semaphore_signal(free_sem.at[u], inc=1, device_id=to_y, device_id_type=MESH)

                    @pl.when(leaf)
                    def _():
                        up.start()

                @act(t0 + keys["p"][2])
                def _(up=up, across=across, kept=kept, z_in=z_in):
                    @pl.when(centre)
                    def _():
                        up.wait_recv()
                        add_into(kept, kept, z_in)
                        across.start()

                @act(t0 + keys["p"][3])
                def _(over=over, across=across, down=down, back_c=back_c, kept=kept, m_in=m_in, out=out,
                      at_kept=at_kept, h=h, u=u):
                    @pl.when(centre)
                    def _():
                        across.wait_recv()
                        add_into(m_in, kept, m_in)
                        down.start()
                        pl.semaphore_wait(free_sem.at[u], 1)
                        back_c.start()
                        emit(m_in, out, at_kept, h, u, 0)

                @act(t0 + keys["p"][4])
                def _(down=down, back_l=back_l, z_in=z_in, out=out, at_kept=at_kept, h=h, u=u):
                    @pl.when(leaf)
                    def _():
                        down.wait_recv()
                        pl.semaphore_wait(free_sem.at[u], 1)
                        back_l.start()
                        emit(z_in, out, at_kept, h, u, 0)

                @act(t0 + keys["p"][5])
                def _(over=over, back_c=back_c, away=away, out=out, at_away=at_away, h=h, u=u):
                    back_c.wait_recv()
                    emit(away, out, at_away, h, u, 1)

                def end(swap=swap, made=made, up=up, across=across, down=down, back_c=back_c, m_in=m_in, away=away,
                        out=out, at_kept=at_kept, at_away=at_away, h=h, u=u):
                    for args in ((m_in, out, at_kept, h, u, 0), (away, out, at_away, h, u, 1)):
                        for copy in both_outputs(*args):
                            copy.wait()
                    if not made:
                        swap.wait_send()
                    back_c.wait_send()

                    @pl.when(leaf)
                    def _():
                        up.wait_send()

                    @pl.when(centre)
                    def _():
                        across.wait_send()
                        down.wait_send()
            else:
                at_own, at_other = upper * h, (1 - upper) * h
                own, other = rows_at(at_own, h), rows_at(at_other, h)
                up = remote(acc, rz_in, u, 1, to_z)
                across = remote(acc.at[other], rm_in, u, 2, to_mid)
                over = remote(acc.at[own], ry_in, u, 3, to_y)
                back = remote(ry_in, acc.at[own], u, 4, to_mid)
                down_a = remote(ry_in, rz_in.at[own], u, 5, to_z)
                down_b = remote(acc.at[other], rz_in.at[other], u, 6, to_z)
                emit_own = (out, mine + at_own, h, u, 0)
                emit_other = (out, mine + at_other, h, u, 1)

                @act(t0 + keys["r"][0])
                def _(gather=gather, up=up):
                    gather()

                    @pl.when(leaf)
                    def _():
                        up.start()

                @act(t0 + keys["r"][1])
                def _(up=up, across=across, acc=acc, rz_in=rz_in):
                    @pl.when(centre)
                    def _():
                        up.wait_recv()
                        add_into(acc, acc, rz_in)
                        across.start()

                @act(t0 + keys["r"][2])
                def _(across=across, over=over, acc=acc, own=own, rm_in=rm_in, u=u):
                    @pl.when(centre)
                    def _():
                        across.wait_recv()
                        add_into(acc.at[own], acc.at[own], rm_in)
                        over.start()
                        across.wait_send()
                        pl.semaphore_signal(free_sem.at[u], inc=1, device_id=to_mid, device_id_type=MESH)

                @act(t0 + keys["r"][3])
                def _(over=over, back=back, down_a=down_a, acc=acc, own=own, ry_in=ry_in, emit_own=emit_own, u=u):
                    @pl.when(centre)
                    def _():
                        over.wait_recv()
                        add_into(ry_in, acc.at[own], ry_in)
                        down_a.start()
                        pl.semaphore_wait(free_sem.at[u], 1)
                        back.start()
                        emit(ry_in, *emit_own)

                @act(t0 + keys["r"][4])
                def _(across=across, back=back, down_b=down_b, acc=acc, other=other, emit_other=emit_other):
                    @pl.when(centre)
                    def _():
                        back.wait_recv()
                        down_b.start()
                        emit(acc.at[other], *emit_other)

                @act(t0 + keys["r"][5])
                def _(down_a=down_a, down_b=down_b, rz_in=rz_in, own=own, other=other, emit_own=emit_own,
                      emit_other=emit_other):
                    @pl.when(leaf)
                    def _():
                        down_a.wait_recv()
                        emit(rz_in.at[own], *emit_own)
                        down_b.wait_recv()
                        emit(rz_in.at[other], *emit_other)

                def end(swap=swap, made=made, up=up, over=over, back=back, down_a=down_a, down_b=down_b, ry_in=ry_in,
                        emit_own=emit_own, emit_other=emit_other):
                    for args in (emit_own, emit_other):
                        for copy in both_outputs(ry_in, *args):
                            copy.wait()
                    if not made:
                        swap.wait_send()

                    @pl.when(leaf)
                    def _():
                        up.wait_send()

                    @pl.when(centre)
                    def _():
                        for copy in (over, back, down_a, down_b):
                            copy.wait_send()

            ends.append(end)

    @act(-1.0)
    def _():
        for load in loads[4:]:
            load.start()

    @act(keys["two"])
    def _():
        for load in loads[:4]:
            load.wait()
        swap_two.wait_recv()
        gain = vec[0:1, :]
        low[pl.ds(tok_rows // 16 * 16, 16), :] = jnp.zeros((16, low.shape[1]), BF16)

        def block(at, carry):
            grad = near[at, :] + far[at, :]
            normal, through = norm_back_rows(after[at, :], grad, gain)
            g_mid = cot[at, :].astype(F32) + through
            mid[at, :] = g_mid
            low[at, :] = g_mid.astype(BF16)
            return tuple(c + fold(v) for c, v in zip(carry, (grad * normal, grad, g_mid)))

        zero = jnp.zeros((1, low.shape[1]), F32)
        sums = each_block(tok_rows, 16, block, (zero, zero, zero))
        small[...] = vec[...]
        for k in range(3):
            small[k + 1 : k + 2, :] = sums[k]

    @act(keys["two"] + 0.001)
    def _():
        loads[4].wait()

        @pl.loop(0, 2)
        def _(i):
            at = pl.ds(pl.multiple_of(i * 256, 256), 256)
            g_heads[at, :] = dot_nt(low[at, :], wproj[...]).astype(BF16)

        for load in loads[5:9]:
            load.wait()

    starts = list(range(0, tok_rows, group))
    lanes = lax.broadcasted_iota(jnp.int32, (1, 128), 1)
    for i, start in enumerate(starts):
        stop = starts[i + 1] if i + 1 < len(starts) else q_s.shape[0]

        @act(keys["attn"][i])
        def _(start=start, size=stop - start):
            rows = pl.ds(start, size)
            first = (lanes < HEAD).astype(F32)

            @pl.loop(0, q_s.shape[1] // 128)
            def _(pair):
                cols = pl.ds(pl.multiple_of(pair * 128, 128), 128)
                live = live_s[rows, pl.ds(0, size)] > 0.0
                grads = attend_back(q_s[rows, cols], k_s[rows, cols], v_s[rows, cols], g_heads[rows, cols], live, first)
                for k in range(3):
                    g_proj[k, rows, cols] = grads[k]

    @act(keys["part"])
    def _():
        for load in loads[9:13]:
            load.wait()
        swap_two.wait_send()

        @pl.loop(0, near.shape[1] // 256)
        def _(i):
            cols = pl.ds(pl.multiple_of(i * 256, 256), 256)
            near[:, cols] = (
                dot_nt(g_proj[0, :tok_rows], wqkv[0, cols, :])
                + dot_nt(g_proj[1, :tok_rows], wqkv[1, cols, :])
                + dot_nt(g_proj[2, :tok_rows], wqkv[2, cols, :])
            )

        swap_one.start()
        zero = jnp.zeros((1, g_proj.shape[2]), F32)
        sums = each_block(
            g_proj.shape[1], 16,
            lambda at, c: tuple(s + fold(g_proj[k, at, :].astype(F32)) for s, k in zip(c, (0, 2))), (zero, zero))
        small[8:9, : g_proj.shape[2]] = sums[0]
        small[8:9, g_proj.shape[2] :] = sums[1]

    own_mlp = pltpu.make_async_copy(mlp_hbm, near, in_sem.at[0])
    put_tok = pltpu.make_async_copy(cot, o_tok, fin_sem.at[0])
    put_layer = pltpu.make_async_copy(tok, o_layer, fin_sem.at[1])

    @act(keys["one"])
    def _():
        swap_one.wait_recv()
        swap_mlp.start()
        gain = vec[9:10, :]

        def block(at, carry):
            grad = near[at, :] + far_one[at, :]
            normal, through = norm_back_rows(tok[at, :].astype(F32), grad, gain)
            cot[at, :] = (mid[at, :] + through).astype(BF16)
            return tuple(c + fold(v) for c, v in zip(carry, (grad * normal, grad)))

        zero = jnp.zeros((1, near.shape[1]), F32)
        sums = each_block(tok_rows, 16, block, (zero, zero))
        for k in range(2):
            small[k + 4 : k + 5, :] = sums[k]
        put_tok.start()
        swap_one.wait_send()
        own_mlp.start()

    @act(keys["layer"])
    def _():
        own_mlp.wait()
        swap_mlp.wait_recv()
        shift = vec[10:11, :]

        def block(at, carry):
            tok[at, :] = (after[at, :] + (near[at, :] + far[at, :]) + shift).astype(BF16)
            return carry

        each_block(tok_rows, 16, block)
        put_layer.start()

    doubles = [
        pltpu.make_async_remote_copy(
            src_ref=small, dst_ref=small_in.at[k], send_sem=v_send.at[k], recv_sem=v_recv.at[k],
            device_id=target, device_id_type=MESH,
        )
        for k, target in enumerate((to_core, to_y, to_z, to_far))
    ]
    for k in range(5):
        @act(keys["small"][k])
        def _(k=k):
            if k:
                doubles[k - 1].wait()
                small[...] = small[...] + small_in[k - 1]
            if k < 4:
                doubles[k].start()
            else:
                put_small.start()

    put_small = pltpu.make_async_copy(small, o_small, fin_sem.at[2])

    for _, _, fn in sorted(actions, key=lambda t: t[:2]):
        fn()
    swap_mlp.wait_send()
    for copy in (put_tok, put_layer, put_small):
        copy.wait()
    for end in ends:
        end()


KEYS = {
    "lag": 0.4, "ahead": 0.8,
    "p": (0, 1, 2, 3, 4, 5), "r": (0, 1.3, 2, 2.7, 3.4, 4.5),
    "two": 3.5, "attn": (3.9, 4.4, 4.9), "part": 5.4, "one": 8.5, "layer": 12.5,
    "small": (12.6, 13, 13.5, 14, 14.5),
}


def backward(args, group, keys=KEYS):
    g_fc2, g_fc1 = args[0], args[1]
    tok_rows, width = args[2].shape
    cols = args[7].shape[1]
    pad_rows = args[7].shape[0]
    shapes = [g_fc2.shape, g_fc1.shape, (width, cols), (cols, width), (width, cols), (width, cols)]
    layout = split_plan(shapes)
    slots, at = [], 0.0
    for m, c, count in layout:
        slots.append([at + j for j in range(count)])
        at += count
    scratch, units = [], 0
    for m, c, count in layout:
        units += 2 * count
        n, h = m // 2, m // 4
        for lead, rows in ((2 * count, n), (count, h), (count, h), (count, h), (count, n), (count, h), (count, h)):
            scratch.append(pltpu.VMEM((lead, rows, c), F32))
    dma = pltpu.SemaphoreType.DMA
    scratch += [
        pltpu.VMEM((tok_rows, width), F32), pltpu.VMEM((tok_rows, width), F32), pltpu.VMEM((tok_rows, width), F32),
        pltpu.VMEM((tok_rows, width), F32), pltpu.VMEM((tok_rows, width), F32), pltpu.VMEM((pad_rows, width), BF16),
        pltpu.VMEM((pad_rows, cols), BF16), pltpu.VMEM((pad_rows, cols), BF16), pltpu.VMEM((pad_rows, cols), BF16),
        pltpu.VMEM((pad_rows, cols), BF16), pltpu.VMEM((3, pad_rows, cols), BF16), pltpu.VMEM((cols, width), BF16),
        pltpu.VMEM((3, width, cols), BF16), pltpu.VMEM((pad_rows, width), BF16), pltpu.VMEM((pad_rows, cols), BF16),
        pltpu.VMEM((tok_rows, width), BF16), pltpu.VMEM((tok_rows, width), BF16), pltpu.VMEM(args[10].shape, F32),
        pltpu.VMEM((16, width), F32), pltpu.VMEM((16, width), F32), pltpu.VMEM((4, 16, width), F32),
        pltpu.VMEM((2, layout[0][0] // 2, layout[0][1]), F32), pltpu.VMEM((2, layout[1][0] // 2, layout[1][1]), F32),
        pltpu.VMEM((2, layout[2][0] // 2, layout[2][1]), F32),
        pltpu.SemaphoreType.REGULAR((units,)), dma((units, 7)), dma((units, 7)), dma((units, 2)), dma((units, 2)), dma((units, 2)),
        dma((13,)), dma((2, 2)), dma((3,)), dma((3,)), dma((4,)), dma((4,)), dma((3,)),
    ]
    spec = pl.BlockSpec(memory_space=pl.ANY)
    shape = jax.ShapeDtypeStruct
    return pl.pallas_call(
        functools.partial(back_kernel, layout, keys, slots, group),
        out_shape=[shape(s, F32) for s in shapes]
        + [shape((tok_rows, width), BF16), shape((tok_rows, width), BF16), shape((16, width), F32)],
        in_specs=[spec] * 16,
        out_specs=[spec] * 9,
        scratch_shapes=scratch,
        name="backward",
        compiler_params=pltpu.CompilerParams(
            collective_id=0, has_side_effects=True, vmem_limit_bytes=67043328
        ),
    )(*args)


def make_body(n_dp, n_mp):
    fast = n_dp == 16 and n_mp == 2

    def sum_mp(part):
        if n_mp == 2:
            return part + swap(part, "mp", 2, 1)
        return lax.psum(part, "mp")

    def body(
        tokens, keep_mask, ln1_gain, ln1_bias, w_qkv, b_qkv, w_proj, b_proj,
        ln2_gain, ln2_bias, w_fc1, b_fc1, w_fc2, b_fc2, cotangent,
    ):
        inputs = tokens.astype(F32)
        tok_rows, width = inputs.shape
        images = keep_mask.shape[0]
        slots = tok_rows // images
        cols = w_qkv.shape[2]
        heads = cols // HEAD
        shape = (images, slots, heads, HEAD)

        if fast:
            group = 4 * slots
            total = -(-tok_rows // group) * group
            kept = jnp.pad(
                jnp.pad((keep_mask > 0).astype(F32).reshape(-1), (0, total - tok_rows)).reshape(-1, group),
                ((0, 8 - total // group), (0, 256 - group)),
            )
            vec = jnp.concatenate(
                [ln2_gain, ln2_bias, b_proj, ln1_bias, b_qkv.reshape(-1), ln1_gain, b_fc1, ln1_gain,
                 ln1_gain, b_fc2]
                + [jnp.zeros(5 * width, F32)]
            ).reshape(16, width)
            weight = w_qkv.transpose(1, 0, 2)
            (norm_one, query, keys, values, heads_out, live_map, after_attn, norm_two, hidden, grad_pre,
             norm_two_part, mlp_part, vec) = front(
                (tokens, kept, weight, w_proj, w_fc1, w_fc2, cotangent, vec), slots, group, w_fc1.shape[1]
            )
            results = backward(
                (dot_tn(hidden[:tok_rows], cotangent), dot_tn(norm_two, grad_pre), norm_two_part, mlp_part,
                 after_attn, tokens, cotangent, query, keys, values, live_map, w_proj, weight, norm_one,
                 heads_out, vec),
                group,
            )
            grad_w_fc2, grad_w_fc1, grad_w_v, grad_w_proj, grad_w_q, grad_w_k = results[:6]
            layer_out, grad_tokens, small = results[6:]
            return (
                layer_out,
                grad_tokens,
                small[4],
                small[5],
                jnp.stack([grad_w_q, grad_w_k, grad_w_v], axis=1),
                small[8].reshape(2, cols),
                grad_w_proj,
                small[3],
                small[1],
                small[2],
                grad_w_fc1,
                small[6:8].reshape(-1),
                grad_w_fc2,
                small[11],
            )

        normal_one, inverse_one = norm_parts(inputs)
        norm_one = (normal_one * ln1_gain + ln1_bias).astype(BF16)
        weight = w_qkv.transpose(1, 0, 2)
        query = (dot_nn(norm_one, weight[0]) + b_qkv[0]).astype(BF16).reshape(shape)
        keys = dot_nn(norm_one, weight[1]).astype(BF16).reshape(shape)
        values = (dot_nn(norm_one, weight[2]) + b_qkv[1]).astype(BF16).reshape(shape)
        scores = jnp.einsum("bqhd,bkhd->bhqk", query, keys, preferred_element_type=F32) * 0.125
        live = (keep_mask > 0)[:, None, None, :]
        masked = jnp.where(live, scores, -1e30)
        row_max = jnp.max(masked, axis=-1, keepdims=True)
        exp_terms = jnp.where(live, jnp.exp(masked - row_max), 0.0)
        probs = exp_terms / jnp.sum(exp_terms, axis=-1, keepdims=True)
        probs_low = probs.astype(BF16)
        mixed = jnp.einsum("bhqk,bkhd->bqhd", probs_low, values, preferred_element_type=F32)
        heads_out = mixed.reshape(tok_rows, cols).astype(BF16)
        after_attn = inputs + sum_mp(dot_nn(heads_out, w_proj)) + b_proj

        normal_two, inverse_two = norm_parts(after_attn)
        norm_two = (normal_two * ln2_gain + ln2_bias).astype(BF16)
        pre_act = dot_nn(norm_two, w_fc1) + b_fc1
        hidden_f, gelu_back = jax.vjp(lambda v: jax.nn.gelu(v, approximate=False), pre_act)
        hidden = hidden_f.astype(BF16)
        grad_w_fc2 = dot_tn(hidden, cotangent)
        grad_pre = gelu_back(dot_nt(cotangent, w_fc2))[0].astype(BF16)
        norm_two_part = dot_nt(grad_pre, w_fc1)
        grad_w_fc1 = dot_tn(norm_two, grad_pre)
        mlp_part = dot_nn(hidden, w_fc2)
        grad_out = cotangent.astype(F32)
        sum_out = jnp.sum(grad_out, axis=0)
        sum_pre = jnp.sum(grad_pre.astype(F32), axis=0)
        grad_norm_two = sum_mp(norm_two_part)
        layer_out = (after_attn + sum_mp(mlp_part) + b_fc2).astype(BF16)
        grad_mid = grad_out + norm_back(grad_norm_two, normal_two, inverse_two, ln2_gain)
        grad_mid_low = grad_mid.astype(BF16)
        grad_heads = dot_nt(grad_mid_low, w_proj).astype(BF16).reshape(shape)
        grad_w_proj = dot_tn(heads_out, grad_mid_low)
        grad_probs = jnp.einsum("bqhd,bkhd->bhqk", grad_heads, values, preferred_element_type=F32)
        grad_values = jnp.einsum(
            "bhqk,bqhd->bkhd", probs_low, grad_heads, preferred_element_type=F32
        ).astype(BF16)
        inner = jnp.sum(probs * grad_probs, axis=-1, keepdims=True)
        grad_scores = (probs * (grad_probs - inner)).astype(BF16)
        grad_query = (
            jnp.einsum("bhqk,bkhd->bqhd", grad_scores, keys, preferred_element_type=F32) * 0.125
        ).astype(BF16)
        grad_keys = (
            jnp.einsum("bhqk,bqhd->bkhd", grad_scores, query, preferred_element_type=F32) * 0.125
        ).astype(BF16)
        grad_query = grad_query.reshape(tok_rows, cols)
        grad_keys = grad_keys.reshape(tok_rows, cols)
        grad_values = grad_values.reshape(tok_rows, cols)
        part = (
            dot_nt(grad_query, weight[0])
            + dot_nt(grad_keys, weight[1])
            + dot_nt(grad_values, weight[2])
        )
        grad_norm_one = sum_mp(part)
        grads = [
            grad_w_fc2,
            grad_w_fc1,
            grad_w_proj,
            dot_tn(norm_one, grad_values),
            dot_tn(norm_one, grad_query),
            dot_tn(norm_one, grad_keys),
        ]
        grads = lax.psum(grads, "dp")
        grad_w_fc2, grad_w_fc1, grad_w_proj, grad_w_v, grad_w_q, grad_w_k = grads
        grad_w_qkv = jnp.stack([grad_w_q, grad_w_k, grad_w_v], axis=1)
        grad_tokens = (
            grad_mid + norm_back(grad_norm_one, normal_one, inverse_one, ln1_gain)
        ).astype(BF16)

        small = jnp.concatenate(
            [
                sum_out,
                jnp.sum(grad_norm_two * normal_two, axis=0),
                jnp.sum(grad_norm_two, axis=0),
                jnp.sum(grad_mid, axis=0),
                jnp.sum(grad_norm_one * normal_one, axis=0),
                jnp.sum(grad_norm_one, axis=0),
                sum_pre,
                jnp.sum(grad_query.astype(F32), axis=0),
                jnp.sum(grad_values.astype(F32), axis=0),
            ]
        )
        small = lax.psum(small, "dp")
        rows = [small[k * width : (k + 1) * width] for k in range(6)]
        spot = 6 * width + b_fc1.shape[0]
        return (
            layer_out,
            grad_tokens,
            rows[4],
            rows[5],
            grad_w_qkv,
            small[spot:].reshape(2, cols),
            grad_w_proj,
            rows[3],
            rows[1],
            rows[2],
            grad_w_fc1,
            small[6 * width : spot],
            grad_w_fc2,
            rows[0],
        )

    return body


def solution(mesh):
    return jax.shard_map(
        make_body(mesh.shape["dp"], mesh.shape["mp"]),
        mesh=mesh,
        in_specs=(
            P("dp", None),
            P("dp", None),
            P(),
            P(),
            P(None, None, "mp"),
            P(None, "mp"),
            P("mp", None),
            P(),
            P(),
            P(),
            P(None, "mp"),
            P("mp"),
            P("mp", None),
            P(),
            P("dp", None),
        ),
        out_specs=(
            P("dp", None),
            P("dp", None),
            P(),
            P(),
            P(None, None, "mp"),
            P(None, "mp"),
            P("mp", None),
            P(),
            P(),
            P(),
            P(None, "mp"),
            P("mp"),
            P("mp", None),
            P(),
        ),
        check_vma=False,
    )
```
